32 devices in a mesh: shot: 8 (over y, x, core), depth: 4 (over z).
Axes of the slice: x: 2, y: 2, z: 4, core: 2. Of those that a mesh axis runs over, the one named last changes fastest.
Arguments:
- probes: bfloat16 [8, 64, 128, 128], P('shot', None, 'depth'), may hold values from -6 to 6
- courant: float32 [128, 128], P('depth'), may hold values from 0.1 to 0.45
- sketches: float32 [8, 128, 64], replicated, may hold values from -0.5 to 0.5
Outputs:
- basis: float32 [64, 128, 128], P(None, 'depth')
- cores: float32 [8, 64, 64], P('shot')
The draws below stay inside these ranges and needn't reach their ends.
All inputs are finite; a program needn't handle non-finite values.
Results may differ from the reference program's by a relative error of at most 0.0003.
Values may be sent and summed in bfloat16 or wider, within the bound.
A program may use at most 64 MiB of HBM per device.

```python
import math
import jax
import jax.numpy as jnp
from jax import lax

R = 64
NX = 128
STEPS = 4
SHOTS = 8
NZ = 128


def draw_probes(key, part):
    key_shot = jax.random.fold_in(key, 11)
    key_probe = jax.random.fold_in(key, 23)
    key_single = jax.random.fold_in(key, 37)
    per_shot = jax.random.normal(key_shot, (SHOTS, 1, NZ, NX), jnp.float32)
    per_probe = jax.random.normal(key_probe, (1, R, NZ, NX), jnp.float32)
    single = jax.random.normal(key_single, (SHOTS, R, NZ, NX), jnp.float32)
    mixture = 0.35 * per_shot + 0.45 * per_probe + 0.8216 * single
    return jnp.clip(mixture, -6.0, 6.0).astype(jnp.bfloat16)


def shard_levels(key, dims, pieces, low, top_value):
    level, own = 1.0, jax.random.fold_in(key, 6)
    for dim, shards_of in pieces:
        steps = jnp.exp(jax.random.uniform(jax.random.fold_in(own, dim), (shards_of,), jnp.float32, low / len(pieces), top_value / len(pieces)))
        level = level * jnp.repeat(steps, dims[dim] // shards_of).reshape([-1 if axis == dim else 1 for axis in range(len(dims))])
    return level


def gaussian(rng, shape, spread, bound, dtype=jnp.bfloat16):
    result = jax.random.normal(rng, shape, jnp.float32) * spread
    return jnp.minimum(jnp.maximum(result, -bound), bound).astype(dtype)


def setup_inputs(seed: int = 0) -> dict:
    seeds = jax.random.split(jax.random.key(seed), 4)
    probes = draw_probes(jax.random.fold_in(seeds[3], 71), 0)
    courant = jnp.clip(0.1 + 0.35 * jax.random.uniform(seeds[1], (NZ, NX), jnp.float32) ** shard_levels(seeds[1], (NZ, NX), ((0, 4),), -0.2, 0.2), 0.1, 0.45)
    sketches = gaussian(seeds[2], (SHOTS, 2 * R, R), (2 * R) ** -0.5, 0.5, jnp.float32)
    return dict(probes=probes, courant=courant, sketches=sketches)


def propagate(field, courant):
    earlier = field
    current = field
    for repeat in range(STEPS):
        padded = jnp.pad(current, ((0, 0), (1, 1), (1, 1)))
        laplace = padded[:, 2:, 1:-1] + padded[:, :-2, 1:-1] + padded[:, 1:-1, 2:] + padded[:, 1:-1, :-2] - 4.0 * current
        earlier, current = (current, 2.0 * current - earlier + courant * laplace)
    return current

def orthonormal(matrix):
    gram = jnp.dot(matrix, matrix.T, precision=lax.Precision.HIGHEST)
    lower_factor = jnp.linalg.cholesky(gram)
    return lax.linalg.triangular_solve(lower_factor, matrix, left_side=True, lower=True)

def response(probes, courant, shot_index):
    field = propagate(probes[shot_index].astype(jnp.float32), courant)
    return field.reshape(R, NZ * NX)

def merge_range(probes, courant, sketches, begin_at, end_at):
    if end_at - begin_at == 1:
        return orthonormal(response(probes, courant, begin_at))
    middle = (begin_at + end_at) // 2
    low_factor = merge_range(probes, courant, sketches, begin_at, middle)
    high_factor = merge_range(probes, courant, sketches, middle, end_at)
    sketch = sketches[middle - 1]
    mixed = jnp.dot(sketch[:R].T, low_factor, precision=lax.Precision.HIGHEST) + jnp.dot(sketch[R:].T, high_factor, precision=lax.Precision.HIGHEST)
    return orthonormal(mixed)

def reference(probes, courant, sketches):
    root = merge_range(probes, courant, sketches, 0, SHOTS)

    def project(shot_probes):
        field = propagate(shot_probes.astype(jnp.float32), courant).reshape(R, NZ * NX)
        return jnp.dot(root, field.T, precision=lax.Precision.HIGHEST) / math.sqrt(R)
    cores = lax.map(project, probes)
    return (root.reshape(R, NZ, NX), cores)
```

```python
import functools
import math

import jax
import jax.numpy as jnp
from jax import lax
from jax.experimental import pallas as pl
from jax.experimental.pallas import tpu as pltpu
from jax.sharding import PartitionSpec as P

STEPS = 4
MESH = pl.DeviceIdType.MESH
HI = lax.Precision.HIGHEST
NN = (((1,), (0,)), ((), ()))
NT = (((1,), (1,)), ((), ()))
TN = (((0,), (0,)), ((), ()))
PIECES = 2
WIDTH = 8


def mm(a, b, dims=NN):
    return lax.dot_general(a, b, dims, precision=HI, preferred_element_type=jnp.float32)


def split(x):
    top = x.astype(jnp.bfloat16)
    return top, (x - top.astype(jnp.float32)).astype(jnp.bfloat16)


def mm3(a, b, dims=NN):
    def part(p, q):
        return lax.dot_general(p, q, dims, preferred_element_type=jnp.float32)

    return part(a[0], b[0]) + (part(a[0], b[1]) + part(a[1], b[0]))


def wide(ref, h, d, picked=slice(None)):
    return jnp.concatenate([ref[h, d + i, picked] for i in range(WIDTH)], axis=1)


def inverse_factor(gram):
    n = gram.shape[0]
    rows = lax.broadcasted_iota(jnp.int32, (n, 1), 0)
    eye = (
        lax.broadcasted_iota(jnp.int32, (n, n), 0) == lax.broadcasted_iota(jnp.int32, (n, n), 1)
    ).astype(jnp.float32)
    a = jnp.concatenate([gram, eye], axis=1)
    blocks = [a[8 * b : 8 * b + 8] for b in range(n // 8)]
    for k in range(0, n, 2):
        b0, r = divmod(k, 8)
        first, second = blocks[b0][r : r + 1], blocks[b0][r + 1 : r + 2]
        p, q, s = first[:, k : k + 1], second[:, k : k + 1], second[:, k + 1 : k + 2]
        if k == n - 2:
            break
        scale = 1.0 / (p * s - q * q)
        row0 = (s * first - q * second) * scale
        row1 = (p * second - q * first) * scale
        for b in range((k + 2) // 8, n // 8):
            col0, col1 = blocks[b][:, k : k + 1], blocks[b][:, k + 1 : k + 2]
            if b == b0:
                below = rows[:8] > r + 1
                col0, col1 = jnp.where(below, col0, 0.0), jnp.where(below, col1, 0.0)
            blocks[b] = blocks[b] - (col0 * row0 + col1 * row1)
    a = jnp.concatenate(blocks, axis=0)
    before = jnp.concatenate([a[n - 1 :], a[: n - 1]], axis=0)
    even = lax.rem(rows, 2) == 0
    own = jnp.sum(a[:, :n] * eye, axis=1, keepdims=True)
    shifted = jnp.concatenate([eye[n - 1 :], eye[: n - 1]], axis=0)
    side = jnp.sum(a[:, :n] * shifted, axis=1, keepdims=True)
    above = jnp.sum(before[:, :n] * shifted, axis=1, keepdims=True)
    ratio = jnp.where(even, 0.0, side / jnp.where(even, 1.0, above))
    value = own - ratio * side
    return (a[:, n:] - ratio * before[:, n:]) * (1.0 / jnp.sqrt(value))


def kernel(
    depths,
    levels,
    probes,
    speed,
    sketches,
    basis,
    cores,
    halo,
    wide_speed,
    field_a,
    field_b,
    pairs,
    sums,
    sums_in,
    halo_send,
    halo_recv,
    speed_send,
    speed_recv,
    pair_send,
    pair_recv,
    sum_send,
    sum_recv,
):
    rows, rank, cells = probes.shape
    shot = lax.axis_index("shot")
    depth = lax.axis_index("depth")
    low_end = depth == 0
    high_end = depth == depths - 1

    def bit(h):
        return lax.rem(shot // (2**h), 2)

    def peer(h):
        return shot + 2**h - 2 ** (h + 1) * bit(h)

    barrier = pltpu.get_barrier_semaphore()
    for h in range(levels):
        pl.semaphore_signal(barrier, inc=1, device_id=(peer(h), depth), device_id_type=MESH)
    for j in range(1, depths):
        other = lax.rem(depth + j, depths)
        pl.semaphore_signal(barrier, inc=1, device_id=(shot, other), device_id_type=MESH)
    pl.semaphore_wait(barrier, levels + depths - 1)

    def halo_copies(side):
        to = depth + 1 if side == 0 else depth - 1
        rows_out = pl.ds(rows - STEPS, STEPS) if side == 0 else pl.ds(0, STEPS)
        first = pltpu.make_async_remote_copy(
            src_ref=probes.at[rows_out],
            dst_ref=halo.at[side],
            send_sem=halo_send.at[side],
            recv_sem=halo_recv.at[side],
            device_id=(shot, to),
            device_id_type=MESH,
        )
        at = 0 if side == 0 else STEPS + rows
        second = pltpu.make_async_remote_copy(
            src_ref=speed.at[rows_out],
            dst_ref=wide_speed.at[pl.ds(at, STEPS)],
            send_sem=speed_send.at[side],
            recv_sem=speed_recv.at[side],
            device_id=(shot, to),
            device_id_type=MESH,
        )
        return first, second

    @pl.when(depth < depths - 1)
    def _():
        for c in halo_copies(0):
            c.start()

    @pl.when(depth > 0)
    def _():
        for c in halo_copies(1):
            c.start()

    @pl.loop(0, rows, unroll=4)
    def _(d):
        field_a[STEPS + d] = probes[d].astype(jnp.float32)

    wide_speed[STEPS : STEPS + rows] = speed[...]

    @pl.when(depth > 0)
    def _():
        for c in halo_copies(0):
            c.wait_recv()
        field_a[0:STEPS] = halo[0].astype(jnp.float32)

    @pl.when(depth == 0)
    def _():
        field_a[0:STEPS] = jnp.zeros((STEPS, rank, cells), jnp.float32)
        wide_speed[0:STEPS] = jnp.zeros((STEPS, cells), jnp.float32)

    @pl.when(depth < depths - 1)
    def _():
        for c in halo_copies(1):
            c.wait_recv()
        field_a[STEPS + rows : 2 * STEPS + rows] = halo[1].astype(jnp.float32)

    @pl.when(depth == depths - 1)
    def _():
        field_a[STEPS + rows : 2 * STEPS + rows] = jnp.zeros((STEPS, rank, cells), jnp.float32)
        wide_speed[STEPS + rows : 2 * STEPS + rows] = jnp.zeros((STEPS, cells), jnp.float32)

    lane = lax.broadcasted_iota(jnp.int32, (rank, cells), 1)
    not_first = lane > 0
    not_last = lane < cells - 1
    me = bit(0)
    mine = pl.ds(pl.multiple_of(me * rank, rank), rank)

    def update(d, source, older):
        u = source[d]
        left = jnp.where(not_first, pltpu.roll(u, 1, 1), 0.0)
        right = jnp.where(not_last, pltpu.roll(u, cells - 1, 1), 0.0)
        laplace = source[d + 1] + source[d - 1] + right + left - 4.0 * u
        return 2.0 * u - older + wide_speed[pl.ds(d, 1)] * laplace

    for step in range(STEPS):
        source, target = (field_a, field_b) if step % 2 == 0 else (field_b, field_a)
        last = step == STEPS - 1

        @pl.loop(step + 1, 2 * STEPS + rows - step - 1, unroll=2)
        def _(d):
            older = source[d] if step == 0 else target[d]
            new = update(d, source, older)
            if last:
                pairs[0, d - STEPS, mine] = new
            else:
                target[d] = new

    def pair_copy(h):
        own = pl.ds(pl.multiple_of(bit(h) * rank, rank), rank)
        return [
            pltpu.make_async_remote_copy(
                src_ref=pairs.at[h, :, own],
                dst_ref=pairs.at[h, :, own],
                send_sem=pair_send.at[h, 0, 0],
                recv_sem=pair_recv.at[h, 0, 0],
                device_id=(peer(h), depth),
                device_id_type=MESH,
            )
        ]

    for c in pair_copy(0):
        c.start()
    for c in pair_copy(0):
        c.wait()

    def gram_body(d, total):
        x = split(wide(pairs, 0, d * WIDTH))
        return total + mm3(x, x, NT)

    zero = jnp.zeros((2 * rank, 2 * rank), jnp.float32)
    gram = lax.fori_loop(0, rows // WIDTH, gram_body, zero)

    def sum_copy(h, j):
        other = lax.rem(depth + j, depths)
        size = 2 * rank if h == 0 else rank
        return pltpu.make_async_remote_copy(
            src_ref=sums.at[h, pl.ds(0, size)],
            dst_ref=sums_in.at[h, depth, pl.ds(0, size)],
            send_sem=sum_send.at[h, j],
            recv_sem=sum_recv.at[h, j],
            device_id=(shot, other),
            device_id_type=MESH,
        )

    def depth_sum(h, value):
        size = value.shape[0]
        sums[h, 0:size] = value
        for j in range(1, depths):
            sum_copy(h, j).start()
        for j in range(1, depths):
            sum_copy(h, j).wait()
        total = None
        for j in range(depths):
            part = jnp.where(depth == j, value, sums_in[h, j, 0:size])
            total = part if total is None else total + part
        return total

    for h in range(levels):
        sums_in[h, depth] = jnp.zeros((2 * rank, 2 * rank), jnp.float32)
    gram = depth_sum(0, gram)

    low = inverse_factor(gram[:rank, :rank])
    high = inverse_factor(gram[rank:, rank:])
    sketch = sketches[shot // 2 * 2]
    mixer = jnp.concatenate(
        [mm(sketch[:rank], low, TN), mm(sketch[rank:], high, TN)], axis=1
    )
    carried = mm(mixer, gram)
    inverse = inverse_factor(mm(carried, mixer, NT))
    mixer = mm(inverse, mixer)
    carried = mm(inverse, carried)
    projected = jnp.where(me == 0, carried[:, :rank], carried[:, rank:])

    for h in range(1, levels):
        own_bit = bit(h)
        own = pl.ds(pl.multiple_of(own_bit * rank, rank), rank)

        parts = split(mixer)
        part_rows = rows // 2**h
        per = part_rows // PIECES
        got = pl.ds(pl.multiple_of((1 - own_bit) * rank, rank), rank)

        def part_at(mask, i):
            part = 0
            for b in range(h):
                part += 2**b * (1 - bit(b) if mask >> b & 1 else bit(b))
            return pl.ds(part * part_rows + i * per, per)

        def part_copy(mask, i):
            low = mask & -mask
            at = part_at(mask - low, i)
            lanes = got if mask else own
            return pltpu.make_async_remote_copy(
                src_ref=pairs.at[h, at, lanes],
                dst_ref=pairs.at[h, at, lanes],
                send_sem=pair_send.at[h, mask, i],
                recv_sem=pair_recv.at[h, mask, i],
                device_id=(peer(low.bit_length() - 1 if mask else h), depth),
                device_id_type=MESH,
            )

        chunks = rows // WIDTH
        ahead = max(1, part_rows // WIDTH)
        first = part_at(0, 0).start // WIDTH
        for t in range(chunks):
            at = lax.rem(first + t, chunks) * WIDTH
            out = mm3(parts, split(wide(pairs, h - 1, at)))
            for w in range(WIDTH):
                pairs[h, at + w, own] = out[:, w * cells : (w + 1) * cells]
            if per == WIDTH and t < PIECES:
                part_copy(0, t).start()
            elif per != WIDTH and t == ahead - 1:
                for i in range(PIECES):
                    part_copy(0, i).start()
        masks = sorted(range(2**h), key=lambda m: (m.bit_count(), -m))
        for mask in masks:
            low = mask & -mask if mask else 2**h
            for i in range(PIECES):
                part_copy(mask, i).wait_recv()
                for b in reversed(range(low.bit_length() - 1)):
                    part_copy(mask + 2**b, i).start()
        for mask in masks:
            for i in range(PIECES):
                part_copy(mask, i).wait_send()

        def cross_body(d, total):
            y = split(wide(pairs, h, d * WIDTH))
            r = split(wide(pairs, 0, d * WIDTH, mine))
            right = [jnp.concatenate([p[rank:], q], axis=0) for p, q in zip(y, r)]
            return total + mm3(y, right, NT)

        cross = lax.fori_loop(0, rows // WIDTH, cross_body, zero)
        value = jnp.concatenate(
            [
                cross[:rank, :rank],
                jnp.where(own_bit == 0, cross[rank:, rank:], cross[:rank, rank:]),
            ],
            axis=1,
        )
        value = depth_sum(h, value)
        stride = 2**h
        sketch = sketches[shot // (2 * stride) * (2 * stride) + stride - 1]
        top, bottom = sketch[:rank], sketch[rank:]
        across = value[:, :rank]
        mixed = mm(sketch, sketch, TN)
        mixed += mm(top, mm(across, bottom), TN) + mm(bottom, mm(across, top, TN), TN)
        inverse = inverse_factor(mixed)
        mixer = mm(inverse, sketch, NT)
        other = value[:, rank:]
        low_part = jnp.where(own_bit == 0, projected, other)
        high_part = jnp.where(own_bit == 0, other, projected)
        projected = mm(mixer, jnp.concatenate([low_part, high_part], axis=0))

    parts = split(mixer)

    @pl.loop(0, rows // WIDTH)
    def _(i):
        out = mm3(parts, split(wide(pairs, levels - 1, i * WIDTH)))
        for w in range(WIDTH):
            basis[i * WIDTH + w] = out[:, w * cells : (w + 1) * cells]

    cores[...] = projected * (1.0 / math.sqrt(rank))

    @pl.when(depth < depths - 1)
    def _():
        for c in halo_copies(0):
            c.wait_send()

    @pl.when(depth > 0)
    def _():
        for c in halo_copies(1):
            c.wait_send()


def body(probes, courant, sketches):
    depths = lax.axis_size("depth")
    levels = lax.axis_size("shot").bit_length() - 1
    local = jnp.transpose(probes[0], (1, 0, 2))
    rows, rank, cells = local.shape
    f32 = jnp.float32
    vmem = pl.BlockSpec(memory_space=pltpu.VMEM)
    dma = pltpu.SemaphoreType.DMA
    basis, cores = pl.pallas_call(
        functools.partial(kernel, depths, levels),
        out_shape=(
            jax.ShapeDtypeStruct((rows, rank, cells), f32),
            jax.ShapeDtypeStruct((rank, rank), f32),
        ),
        in_specs=[vmem] * 3,
        out_specs=(vmem, vmem),
        scratch_shapes=[
            pltpu.VMEM((2, STEPS, rank, cells), jnp.bfloat16),
            pltpu.VMEM((rows + 2 * STEPS, cells), f32),
            pltpu.VMEM((rows + 2 * STEPS, rank, cells), f32),
            pltpu.VMEM((rows + 2 * STEPS, rank, cells), f32),
            pltpu.VMEM((levels, rows, 2 * rank, cells), f32),
            pltpu.VMEM((levels, 2 * rank, 2 * rank), f32),
            pltpu.VMEM((levels, depths, 2 * rank, 2 * rank), f32),
            dma((2,)),
            dma((2,)),
            dma((2,)),
            dma((2,)),
            dma((levels, 2 ** (levels - 1), PIECES)),
            dma((levels, 2 ** (levels - 1), PIECES)),
            dma((levels, depths)),
            dma((levels, depths)),
        ],
        compiler_params=pltpu.CompilerParams(
            collective_id=0, has_side_effects=True, vmem_limit_bytes=56 * 2**20
        ),
    )(local, courant, sketches)
    return (jnp.transpose(basis, (1, 0, 2)), cores[None])


def choose(bit_value, low, high):
    return jnp.where(bit_value == 0, low, high)


def merged(sketch, near, theirs):
    half = mm(
        jnp.concatenate([0.5 * sketch, near], axis=1),
        jnp.concatenate([sketch, theirs], axis=1),
        NT,
    )
    return half + jnp.transpose(half)


def plane_kernel(
    depths,
    probes,
    speed,
    sketches,
    basis,
    cores,
    halo,
    wide_speed,
    field_a,
    field_b,
    pair,
    whole,
    first_sum,
    first_in,
    gram_all,
    quad_part,
    quad_in,
    quad_sum,
    quad_depth,
    quad_all,
    root_part,
    root_in,
    root_sum,
    root_depth,
    root_all,
    quad_mixer,
    quad_mixer_in,
    root_mixer,
    root_mixer_in,
    gathered,
    send_sems,
    recv_sems,
    local_sems,
):
    rows, rank, cells = probes.shape
    shots = 8
    per = rows // shots
    part = 2 * rank // 4
    shot = lax.axis_index("shot")
    depth = lax.axis_index("depth")

    def bit(h, of=shot):
        return lax.rem(of // (2**h), 2)

    def flip(mask, of=shot):
        value = 0
        for h in range(3):
            value += 2**h * (1 - bit(h, of) if mask >> h & 1 else bit(h, of))
        return value

    core, low_x, low_y = bit(0), bit(1), bit(2)

    barrier = pltpu.get_barrier_semaphore()
    for mask in range(1, shots):
        pl.semaphore_signal(barrier, inc=1, device_id=(flip(mask), depth), device_id_type=MESH)
    for j in range(1, depths):
        other = lax.rem(depth + j, depths)
        pl.semaphore_signal(barrier, inc=1, device_id=(shot, other), device_id_type=MESH)
    pl.semaphore_wait(barrier, shots - 1 + depths - 1)

    used = [0]

    def take(count):
        used[0] += count
        return used[0] - count

    def copy(src, dst, sem, to):
        return pltpu.make_async_remote_copy(
            src_ref=src,
            dst_ref=dst,
            send_sem=send_sems.at[sem],
            recv_sem=recv_sems.at[sem],
            device_id=to,
            device_id_type=MESH,
        )

    halo_sem, speed_sem = take(2), take(2)

    def halo_copies(side):
        to = depth + 1 if side == 0 else depth - 1
        rows_out = pl.ds(rows - STEPS, STEPS) if side == 0 else pl.ds(0, STEPS)
        at = 0 if side == 0 else STEPS + rows
        return (
            copy(probes.at[rows_out], halo.at[side], halo_sem + side, (shot, to)),
            copy(
                speed.at[rows_out],
                wide_speed.at[pl.ds(at, STEPS)],
                speed_sem + side,
                (shot, to),
            ),
        )

    @pl.when(depth < depths - 1)
    def _():
        for c in halo_copies(0):
            c.start()

    @pl.when(depth > 0)
    def _():
        for c in halo_copies(1):
            c.start()

    @pl.loop(0, rows, unroll=4)
    def _(d):
        field_a[STEPS + d] = probes[d].astype(jnp.float32)

    wide_speed[STEPS : STEPS + rows] = speed[...]

    @pl.when(depth > 0)
    def _():
        for c in halo_copies(0):
            c.wait_recv()
        field_a[0:STEPS] = halo[0].astype(jnp.float32)

    @pl.when(depth == 0)
    def _():
        field_a[0:STEPS] = jnp.zeros((STEPS, rank, cells), jnp.float32)
        wide_speed[0:STEPS] = jnp.zeros((STEPS, cells), jnp.float32)

    @pl.when(depth < depths - 1)
    def _():
        for c in halo_copies(1):
            c.wait_recv()
        field_a[STEPS + rows : 2 * STEPS + rows] = halo[1].astype(jnp.float32)

    @pl.when(depth == depths - 1)
    def _():
        field_a[STEPS + rows : 2 * STEPS + rows] = jnp.zeros((STEPS, rank, cells), jnp.float32)
        wide_speed[STEPS + rows : 2 * STEPS + rows] = jnp.zeros((STEPS, cells), jnp.float32)

    lane = lax.broadcasted_iota(jnp.int32, (rank, cells), 1)
    not_first = lane > 0
    not_last = lane < cells - 1
    mine = pl.ds(pl.multiple_of(core * rank, rank), rank)

    def update(d, source, older):
        u = source[d]
        left = jnp.where(not_first, pltpu.roll(u, 1, 1), 0.0)
        right = jnp.where(not_last, pltpu.roll(u, cells - 1, 1), 0.0)
        laplace = source[d + 1] + source[d - 1] + right + left - 4.0 * u
        return 2.0 * u - older + wide_speed[pl.ds(d, 1)] * laplace

    for step in range(STEPS - 1):
        source, target = (field_a, field_b) if step % 2 == 0 else (field_b, field_a)

        @pl.loop(step + 1, 2 * STEPS + rows - step - 1, unroll=2)
        def _(d):
            older = source[d] if step == 0 else target[d]
            target[d] = update(d, source, older)

    pair_sem, spread_sem = take(shots), take(shots)

    def pair_copy(i):
        at = pl.ds(i * per, per)
        return copy(pair.at[at, mine], pair.at[at, mine], pair_sem + i, (flip(1), depth))

    def spread_copy(to, mask):
        at = pl.ds(to * per, per)
        into = pl.ds(pl.multiple_of(shot * rank, rank), rank)
        return copy(pair.at[at, mine], whole.at[:, into], spread_sem + mask, (to, depth))

    source, target = (field_a, field_b) if (STEPS - 1) % 2 == 0 else (field_b, field_a)

    @pl.loop(0, shots)
    def _(i):
        for w in range(per):
            d = STEPS + i * per + w
            pair[i * per + w, mine] = update(d, source, target[d])
        pair_copy(i).start()

        @pl.when(i // 2 != shot // 2)
        def _():
            mask = 0
            for h in range(3):
                mask += 2**h * lax.rem(bit(h, i) + bit(h), 2)
            spread_copy(i, mask).start()

    group = WIDTH // per

    def gram_body(t, total):
        for i in range(group):
            pair_copy(t * group + i).wait_recv()
        at = t * WIDTH
        x = split(jnp.concatenate([pair[at + i] for i in range(WIDTH)], axis=1))
        return total + mm3(x, x, NT)

    zero = jnp.zeros((2 * rank, 2 * rank), jnp.float32)
    gram = lax.fori_loop(0, rows // WIDTH, gram_body, zero)

    def depth_start(source, into, sem):
        for j in range(1, depths):
            other = lax.rem(depth + j, depths)
            copy(source, into.at[depth], sem + j, (shot, other)).start()

    def depth_finish(source, into, sem, value):
        for j in range(1, depths):
            other = lax.rem(depth + j, depths)
            copy(source, into.at[depth], sem + j, (shot, other)).wait_recv()
        total = None
        for j in range(depths):
            one = jnp.where(depth == j, value, into[j])
            total = one if total is None else total + one
        return total

    for into in (first_in, quad_depth, root_depth):
        into[depth] = jnp.zeros(into.shape[1:], jnp.float32)

    first_sem, first_pair_sem = take(depths), take(1)
    half = choose(core, gram[:rank], gram[rank:])
    first_sum[...] = half
    depth_start(first_sum, first_in, first_sem)
    own_rows = pl.ds(pl.multiple_of(shot // 2 * 2 * rank, 2 * rank), 2 * rank)
    for w in range(per):
        whole[w, own_rows] = pair[shot * per + w]
    gram_all[mine] = depth_finish(first_sum, first_in, first_sem, half)
    first_pair = copy(gram_all.at[mine], gram_all.at[mine], first_pair_sem, (flip(1), depth))
    first_pair.start()
    first_pair.wait_recv()
    gram = gram_all[...]

    low = inverse_factor(gram[:rank, :rank])
    high = inverse_factor(gram[rank:, rank:])

    for mask in range(2, shots):
        spread_copy(flip(mask), mask).wait_recv()

    def cross(first, second, size):
        total = None
        for w in range(0, per, 2):
            x = split(jnp.concatenate([whole[w, first : first + size], whole[w + 1, first : first + size]], axis=1))
            y = split(jnp.concatenate([whole[w, second : second + size], whole[w + 1, second : second + size]], axis=1))
            one = mm3(x, y, NT)
            total = one if total is None else total + one
        return total

    quad_sem, quad_depth_sem, quad_all_sem = take(shots), take(depths), take(4)
    root_sem, root_depth_sem, root_all_sem = take(shots), take(depths), take(shots)
    tall = 2 * rank // 4
    for q in range(2):
        value = cross(4 * rank * q, 4 * rank * q + 2 * rank, 2 * rank)
        for i in range(4):
            quad_part[4 * q + i] = value[i * tall : (i + 1) * tall]

    def scatter(source, into, sem, mask):
        return copy(source.at[flip(mask)], into.at[mask], sem + mask, (flip(mask), depth))

    for mask in range(1, shots):
        scatter(quad_part, quad_in, quad_sem, mask).start()
    value = cross(0, 4 * rank, 4 * rank)
    for i in range(shots):
        root_part[i] = value[i * tall : (i + 1) * tall]
    for mask in range(1, shots):
        scatter(root_part, root_in, root_sem, mask).start()

    def scattered(source, into, sem):
        total = source[shot]
        for mask in range(1, shots):
            scatter(source, into, sem, mask).wait_recv()
            total = total + into[mask]
        return total

    def piece_copy(ref, at, sem, mask):
        here = pl.ds(pl.multiple_of(at * tall, tall), tall)
        return copy(ref.at[here], ref.at[here], sem + mask, (flip(mask), depth))

    sketch = sketches[shot // 2 * 2]
    left = mm(sketch[:, :rank], low)
    right = mm(sketch[:, rank:], high)
    mixed = merged(sketch, mm(left, gram[:rank, rank:]), right)

    quad_own = scattered(quad_part, quad_in, quad_sem)
    quad_sum[...] = quad_own
    depth_start(quad_sum, quad_depth, quad_depth_sem)

    inverse = inverse_factor(mixed)
    sketch = sketches[shot // 4 * 4 + 1]
    carry = mm(choose(low_x, sketch[:, :rank], sketch[:, rank:]), inverse)
    mine_quad = mm(carry, jnp.concatenate([left, right], axis=1))
    quad_mixer[...] = mine_quad
    exchange_sem = take(2)
    quad_exchange = copy(quad_mixer, quad_mixer_in, exchange_sem, (flip(2), depth))
    quad_exchange.start()

    quad_at = 2 * low_x + core
    quad_all[pl.ds(pl.multiple_of(quad_at * tall, tall), tall)] = depth_finish(
        quad_sum, quad_depth, quad_depth_sem, quad_own
    )
    for mask in range(1, 4):
        piece_copy(quad_all, quad_at, quad_all_sem, mask).start()
    root_own = scattered(root_part, root_in, root_sem)
    root_sum[...] = root_own
    depth_start(root_sum, root_depth, root_depth_sem)
    for mask in range(1, 4):
        piece_copy(quad_all, quad_at, quad_all_sem, mask).wait_recv()

    quad = quad_all[...]
    near = choose(low_x, mm(mine_quad, quad), mm(mine_quad, quad, NT))
    quad_exchange.wait_recv()
    their_quad = quad_mixer_in[...]
    mixed = merged(sketch, near, their_quad)

    root_all[pl.ds(pl.multiple_of(shot * tall, tall), tall)] = depth_finish(
        root_sum, root_depth, root_depth_sem, root_own
    )
    for mask in range(1, shots):
        piece_copy(root_all, shot, root_all_sem, mask).start()

    inverse = inverse_factor(mixed)
    sketch = sketches[3]
    carry = mm(choose(low_y, sketch[:, :rank], sketch[:, rank:]), inverse)
    joined = jnp.concatenate(
        [
            choose(low_x, mine_quad, their_quad),
            choose(low_x, their_quad, mine_quad),
        ],
        axis=1,
    )
    mine_root = mm(carry, joined)
    root_mixer[...] = mine_root
    root_exchange = copy(root_mixer, root_mixer_in, exchange_sem + 1, (flip(4), depth))
    root_exchange.start()
    for mask in range(1, shots):
        piece_copy(root_all, shot, root_all_sem, mask).wait_recv()

    root = root_all[...]
    near = choose(low_y, mm(mine_root, root), mm(mine_root, root, NT))
    root_exchange.wait_recv()
    their_root = root_mixer_in[...]
    inverse = inverse_factor(merged(sketch, near, their_root))
    mine_root = mm(inverse, mine_root)
    their_root = mm(inverse, their_root)
    mixer = jnp.concatenate(
        [
            choose(low_y, mine_root, their_root),
            choose(low_y, their_root, mine_root),
        ],
        axis=1,
    )

    share_sem = take(2 * shots)
    parts = split(mixer)

    def share_copy(mask, i):
        at = pl.ds(shot * per + 2 * i, 2)
        return copy(gathered.at[at], gathered.at[at], share_sem + 2 * mask + i, (flip(mask), depth))

    def forward_copy(mask, i):
        at = pl.ds(flip(mask) * per + 2 * i, 2)
        return copy(gathered.at[at], gathered.at[at], share_sem + 2 * (mask + 1) + i, (flip(1), depth))

    for i in range(per // 2):
        out = mm3(parts, split(jnp.concatenate([whole[2 * i], whole[2 * i + 1]], axis=1)))
        for w in range(2):
            gathered[shot * per + 2 * i + w] = out[:, w * cells : (w + 1) * cells]
        for mask in (6, 2, 4, 1):
            share_copy(mask, i).start()

    own = choose(low_x, mine_root[:, : 2 * rank], mine_root[:, 2 * rank :])
    other = choose(low_x, mine_root[:, 2 * rank :], mine_root[:, : 2 * rank])
    near = mm(own, gram)
    near += choose(low_x, mm(other, quad, NT), mm(other, quad))
    far = choose(low_y, mm(their_root, root, NT), mm(their_root, root))
    near += choose(low_x, far[:, : 2 * rank], far[:, 2 * rank :])
    cores[...] = choose(core, near[:, :rank], near[:, rank:]) * (1.0 / math.sqrt(rank))

    for i in range(per // 2):
        for mask in (2, 4, 6):
            share_copy(mask, i).wait_recv()
            forward_copy(mask, i).start()
    for i in range(per // 2):
        for mask in (1, 3, 5, 7):
            share_copy(mask, i).wait_recv()

    out_copy = pltpu.make_async_copy(gathered, basis, local_sems.at[0])
    out_copy.start()

    @pl.when(depth < depths - 1)
    def _():
        for c in halo_copies(0):
            c.wait_send()

    @pl.when(depth > 0)
    def _():
        for c in halo_copies(1):
            c.wait_send()

    for i in range(shots):
        pair_copy(i).wait_send()
    for mask in range(2, shots):
        spread_copy(flip(mask), mask).wait_send()
    for source, into, sem in (
        (first_sum, first_in, first_sem),
        (quad_sum, quad_depth, quad_depth_sem),
        (root_sum, root_depth, root_depth_sem),
    ):
        for j in range(1, depths):
            other = lax.rem(depth + j, depths)
            copy(source, into.at[depth], sem + j, (shot, other)).wait_send()
    first_pair.wait_send()
    for mask in range(1, shots):
        scatter(quad_part, quad_in, quad_sem, mask).wait_send()
        scatter(root_part, root_in, root_sem, mask).wait_send()
        piece_copy(root_all, shot, root_all_sem, mask).wait_send()
    for mask in range(1, 4):
        piece_copy(quad_all, quad_at, quad_all_sem, mask).wait_send()
    quad_exchange.wait_send()
    root_exchange.wait_send()
    for i in range(per // 2):
        for mask in (1, 2, 4, 6):
            share_copy(mask, i).wait_send()
        for mask in (2, 4, 6):
            forward_copy(mask, i).wait_send()
    out_copy.wait()
    assert used[0] <= SEMS


SEMS = 112


def plane_body(probes, courant, sketches):
    depths = lax.axis_size("depth")
    shots = lax.axis_size("shot")
    local = jnp.transpose(probes[0], (1, 0, 2))
    rows, rank, cells = local.shape
    per = rows // shots
    tall = rank // 2
    f32 = jnp.float32
    vmem = pl.BlockSpec(memory_space=pltpu.VMEM)
    dma = pltpu.SemaphoreType.DMA

    def scratch(*shape):
        return pltpu.VMEM(shape, f32)

    basis, cores = pl.pallas_call(
        functools.partial(plane_kernel, depths),
        out_shape=(
            jax.ShapeDtypeStruct((rows, rank, cells), f32),
            jax.ShapeDtypeStruct((rank, rank), f32),
        ),
        in_specs=[vmem] * 3,
        out_specs=(pl.BlockSpec(memory_space=pl.ANY), vmem),
        scratch_shapes=[
            pltpu.VMEM((2, STEPS, rank, cells), jnp.bfloat16),
            scratch(rows + 2 * STEPS, cells),
            scratch(rows + 2 * STEPS, rank, cells),
            scratch(rows + 2 * STEPS, rank, cells),
            scratch(rows, 2 * rank, cells),
            scratch(per, shots * rank, cells),
            scratch(rank, 2 * rank),
            scratch(depths, rank, 2 * rank),
            scratch(2 * rank, 2 * rank),
            scratch(shots, tall, 2 * rank),
            scratch(shots, tall, 2 * rank),
            scratch(tall, 2 * rank),
            scratch(depths, tall, 2 * rank),
            scratch(2 * rank, 2 * rank),
            scratch(shots, tall, 4 * rank),
            scratch(shots, tall, 4 * rank),
            scratch(tall, 4 * rank),
            scratch(depths, tall, 4 * rank),
            scratch(4 * rank, 4 * rank),
            scratch(rank, 2 * rank),
            scratch(rank, 2 * rank),
            scratch(rank, 4 * rank),
            scratch(rank, 4 * rank),
            scratch(rows, rank, cells),
            dma((SEMS,)),
            dma((SEMS,)),
            dma((1,)),
        ],
        compiler_params=pltpu.CompilerParams(
            collective_id=0, has_side_effects=True, vmem_limit_bytes=56 * 2**20
        ),
    )(local, courant, jnp.transpose(sketches, (0, 2, 1)))
    return (jnp.transpose(basis, (1, 0, 2)), cores[None])


def solution(mesh):
    placed = (P("shot", None, "depth", None), P("depth", None), P())
    plane = mesh.shape["shot"] == 8
    return jax.shard_map(
        plane_body if plane else body,
        mesh=mesh,
        in_specs=placed,
        out_specs=(P(None, "depth", None), P("shot", None, None)),
        check_vma=False,
    )
```

```python
import functools
import math

import jax
import jax.numpy as jnp
from jax import lax
from jax.experimental import pallas as pl
from jax.experimental.pallas import tpu as pltpu
from jax.sharding import PartitionSpec as P

STEPS = 4
MESH = pl.DeviceIdType.MESH
HI = lax.Precision.HIGHEST
NN = (((1,), (0,)), ((), ()))
NT = (((1,), (1,)), ((), ()))
TN = (((0,), (0,)), ((), ()))
PIECES = 2
WIDTH = 8


def mm(a, b, dims=NN):
    return lax.dot_general(a, b, dims, precision=HI, preferred_element_type=jnp.float32)


def split(x):
    top = x.astype(jnp.bfloat16)
    return top, (x - top.astype(jnp.float32)).astype(jnp.bfloat16)


def mm3(a, b, dims=NN):
    def part(p, q):
        return lax.dot_general(p, q, dims, preferred_element_type=jnp.float32)

    return part(a[0], b[0]) + (part(a[0], b[1]) + part(a[1], b[0]))


def wide(ref, h, d, picked=slice(None)):
    return jnp.concatenate([ref[h, d + i, picked] for i in range(WIDTH)], axis=1)


def inverse_factor(gram):
    n = gram.shape[0]
    rows = lax.broadcasted_iota(jnp.int32, (n, 1), 0)
    eye = (
        lax.broadcasted_iota(jnp.int32, (n, n), 0) == lax.broadcasted_iota(jnp.int32, (n, n), 1)
    ).astype(jnp.float32)
    a = jnp.concatenate([gram, eye], axis=1)
    blocks = [a[8 * b : 8 * b + 8] for b in range(n // 8)]
    for k in range(0, n, 2):
        b0, r = divmod(k, 8)
        first, second = blocks[b0][r : r + 1], blocks[b0][r + 1 : r + 2]
        p, q, s = first[:, k : k + 1], second[:, k : k + 1], second[:, k + 1 : k + 2]
        if k == n - 2:
            break
        scale = 1.0 / (p * s - q * q)
        row0 = (s * first - q * second) * scale
        row1 = (p * second - q * first) * scale
        for b in range((k + 2) // 8, n // 8):
            col0, col1 = blocks[b][:, k : k + 1], blocks[b][:, k + 1 : k + 2]
            if b == b0:
                below = rows[:8] > r + 1
                col0, col1 = jnp.where(below, col0, 0.0), jnp.where(below, col1, 0.0)
            blocks[b] = blocks[b] - (col0 * row0 + col1 * row1)
    a = jnp.concatenate(blocks, axis=0)
    before = jnp.concatenate([a[n - 1 :], a[: n - 1]], axis=0)
    even = lax.rem(rows, 2) == 0
    own = jnp.sum(a[:, :n] * eye, axis=1, keepdims=True)
    shifted = jnp.concatenate([eye[n - 1 :], eye[: n - 1]], axis=0)
    side = jnp.sum(a[:, :n] * shifted, axis=1, keepdims=True)
    above = jnp.sum(before[:, :n] * shifted, axis=1, keepdims=True)
    ratio = jnp.where(even, 0.0, side / jnp.where(even, 1.0, above))
    value = own - ratio * side
    return (a[:, n:] - ratio * before[:, n:]) * (1.0 / jnp.sqrt(value))


def kernel(
    depths,
    levels,
    probes,
    speed,
    sketches,
    basis,
    cores,
    halo,
    wide_speed,
    field_a,
    field_b,
    pairs,
    sums,
    sums_in,
    halo_send,
    halo_recv,
    speed_send,
    speed_recv,
    pair_send,
    pair_recv,
    sum_send,
    sum_recv,
):
    rows, rank, cells = probes.shape
    shot = lax.axis_index("shot")
    depth = lax.axis_index("depth")
    low_end = depth == 0
    high_end = depth == depths - 1

    def bit(h):
        return lax.rem(shot // (2**h), 2)

    def peer(h):
        return shot + 2**h - 2 ** (h + 1) * bit(h)

    barrier = pltpu.get_barrier_semaphore()
    for h in range(levels):
        pl.semaphore_signal(barrier, inc=1, device_id=(peer(h), depth), device_id_type=MESH)
    for j in range(1, depths):
        other = lax.rem(depth + j, depths)
        pl.semaphore_signal(barrier, inc=1, device_id=(shot, other), device_id_type=MESH)
    pl.semaphore_wait(barrier, levels + depths - 1)

    def halo_copies(side):
        to = depth + 1 if side == 0 else depth - 1
        rows_out = pl.ds(rows - STEPS, STEPS) if side == 0 else pl.ds(0, STEPS)
        first = pltpu.make_async_remote_copy(
            src_ref=probes.at[rows_out],
            dst_ref=halo.at[side],
            send_sem=halo_send.at[side],
            recv_sem=halo_recv.at[side],
            device_id=(shot, to),
            device_id_type=MESH,
        )
        at = 0 if side == 0 else STEPS + rows
        second = pltpu.make_async_remote_copy(
            src_ref=speed.at[rows_out],
            dst_ref=wide_speed.at[pl.ds(at, STEPS)],
            send_sem=speed_send.at[side],
            recv_sem=speed_recv.at[side],
            device_id=(shot, to),
            device_id_type=MESH,
        )
        return first, second

    @pl.when(depth < depths - 1)
    def _():
        for c in halo_copies(0):
            c.start()

    @pl.when(depth > 0)
    def _():
        for c in halo_copies(1):
            c.start()

    @pl.loop(0, rows, unroll=4)
    def _(d):
        field_a[STEPS + d] = probes[d].astype(jnp.float32)

    wide_speed[STEPS : STEPS + rows] = speed[...]

    @pl.when(depth > 0)
    def _():
        for c in halo_copies(0):
            c.wait_recv()
        field_a[0:STEPS] = halo[0].astype(jnp.float32)

    @pl.when(depth == 0)
    def _():
        field_a[0:STEPS] = jnp.zeros((STEPS, rank, cells), jnp.float32)
        wide_speed[0:STEPS] = jnp.zeros((STEPS, cells), jnp.float32)

    @pl.when(depth < depths - 1)
    def _():
        for c in halo_copies(1):
            c.wait_recv()
        field_a[STEPS + rows : 2 * STEPS + rows] = halo[1].astype(jnp.float32)

    @pl.when(depth == depths - 1)
    def _():
        field_a[STEPS + rows : 2 * STEPS + rows] = jnp.zeros((STEPS, rank, cells), jnp.float32)
        wide_speed[STEPS + rows : 2 * STEPS + rows] = jnp.zeros((STEPS, cells), jnp.float32)

    lane = lax.broadcasted_iota(jnp.int32, (rank, cells), 1)
    not_first = lane > 0
    not_last = lane < cells - 1
    me = bit(0)
    mine = pl.ds(pl.multiple_of(me * rank, rank), rank)

    def update(d, source, older):
        u = source[d]
        left = jnp.where(not_first, pltpu.roll(u, 1, 1), 0.0)
        right = jnp.where(not_last, pltpu.roll(u, cells - 1, 1), 0.0)
        laplace = source[d + 1] + source[d - 1] + right + left - 4.0 * u
        return 2.0 * u - older + wide_speed[pl.ds(d, 1)] * laplace

    for step in range(STEPS):
        source, target = (field_a, field_b) if step % 2 == 0 else (field_b, field_a)
        last = step == STEPS - 1

        @pl.loop(step + 1, 2 * STEPS + rows - step - 1, unroll=2)
        def _(d):
            older = source[d] if step == 0 else target[d]
            new = update(d, source, older)
            if last:
                pairs[0, d - STEPS, mine] = new
            else:
                target[d] = new

    def pair_copy(h):
        own = pl.ds(pl.multiple_of(bit(h) * rank, rank), rank)
        return [
            pltpu.make_async_remote_copy(
                src_ref=pairs.at[h, :, own],
                dst_ref=pairs.at[h, :, own],
                send_sem=pair_send.at[h, 0, 0],
                recv_sem=pair_recv.at[h, 0, 0],
                device_id=(peer(h), depth),
                device_id_type=MESH,
            )
        ]

    for c in pair_copy(0):
        c.start()
    for c in pair_copy(0):
        c.wait()

    def gram_body(d, total):
        x = split(wide(pairs, 0, d * WIDTH))
        return total + mm3(x, x, NT)

    zero = jnp.zeros((2 * rank, 2 * rank), jnp.float32)
    gram = lax.fori_loop(0, rows // WIDTH, gram_body, zero)

    def sum_copy(h, j):
        other = lax.rem(depth + j, depths)
        size = 2 * rank if h == 0 else rank
        return pltpu.make_async_remote_copy(
            src_ref=sums.at[h, pl.ds(0, size)],
            dst_ref=sums_in.at[h, depth, pl.ds(0, size)],
            send_sem=sum_send.at[h, j],
            recv_sem=sum_recv.at[h, j],
            device_id=(shot, other),
            device_id_type=MESH,
        )

    def depth_sum(h, value):
        size = value.shape[0]
        sums[h, 0:size] = value
        for j in range(1, depths):
            sum_copy(h, j).start()
        for j in range(1, depths):
            sum_copy(h, j).wait()
        total = None
        for j in range(depths):
            part = jnp.where(depth == j, value, sums_in[h, j, 0:size])
            total = part if total is None else total + part
        return total

    for h in range(levels):
        sums_in[h, depth] = jnp.zeros((2 * rank, 2 * rank), jnp.float32)
    gram = depth_sum(0, gram)

    low = inverse_factor(gram[:rank, :rank])
    high = inverse_factor(gram[rank:, rank:])
    sketch = sketches[shot // 2 * 2]
    mixer = jnp.concatenate(
        [mm(sketch[:rank], low, TN), mm(sketch[rank:], high, TN)], axis=1
    )
    carried = mm(mixer, gram)
    inverse = inverse_factor(mm(carried, mixer, NT))
    mixer = mm(inverse, mixer)
    carried = mm(inverse, carried)
    projected = jnp.where(me == 0, carried[:, :rank], carried[:, rank:])

    for h in range(1, levels):
        own_bit = bit(h)
        own = pl.ds(pl.multiple_of(own_bit * rank, rank), rank)

        parts = split(mixer)
        part_rows = rows // 2**h
        per = part_rows // PIECES
        got = pl.ds(pl.multiple_of((1 - own_bit) * rank, rank), rank)

        def part_at(mask, i):
            part = 0
            for b in range(h):
                part += 2**b * (1 - bit(b) if mask >> b & 1 else bit(b))
            return pl.ds(part * part_rows + i * per, per)

        def part_copy(mask, i):
            low = mask & -mask
            at = part_at(mask - low, i)
            lanes = got if mask else own
            return pltpu.make_async_remote_copy(
                src_ref=pairs.at[h, at, lanes],
                dst_ref=pairs.at[h, at, lanes],
                send_sem=pair_send.at[h, mask, i],
                recv_sem=pair_recv.at[h, mask, i],
                device_id=(peer(low.bit_length() - 1 if mask else h), depth),
                device_id_type=MESH,
            )

        chunks = rows // WIDTH
        ahead = max(1, part_rows // WIDTH)
        first = part_at(0, 0).start // WIDTH
        for t in range(chunks):
            at = lax.rem(first + t, chunks) * WIDTH
            out = mm3(parts, split(wide(pairs, h - 1, at)))
            for w in range(WIDTH):
                pairs[h, at + w, own] = out[:, w * cells : (w + 1) * cells]
            if per == WIDTH and t < PIECES:
                part_copy(0, t).start()
            elif per != WIDTH and t == ahead - 1:
                for i in range(PIECES):
                    part_copy(0, i).start()
        masks = sorted(range(2**h), key=lambda m: (m.bit_count(), -m))
        for mask in masks:
            low = mask & -mask if mask else 2**h
            for i in range(PIECES):
                part_copy(mask, i).wait_recv()
                for b in reversed(range(low.bit_length() - 1)):
                    part_copy(mask + 2**b, i).start()
        for mask in masks:
            for i in range(PIECES):
                part_copy(mask, i).wait_send()

        def cross_body(d, total):
            y = split(wide(pairs, h, d * WIDTH))
            r = split(wide(pairs, 0, d * WIDTH, mine))
            right = [jnp.concatenate([p[rank:], q], axis=0) for p, q in zip(y, r)]
            return total + mm3(y, right, NT)

        cross = lax.fori_loop(0, rows // WIDTH, cross_body, zero)
        value = jnp.concatenate(
            [
                cross[:rank, :rank],
                jnp.where(own_bit == 0, cross[rank:, rank:], cross[:rank, rank:]),
            ],
            axis=1,
        )
        value = depth_sum(h, value)
        stride = 2**h
        sketch = sketches[shot // (2 * stride) * (2 * stride) + stride - 1]
        top, bottom = sketch[:rank], sketch[rank:]
        across = value[:, :rank]
        mixed = mm(sketch, sketch, TN)
        mixed += mm(top, mm(across, bottom), TN) + mm(bottom, mm(across, top, TN), TN)
        inverse = inverse_factor(mixed)
        mixer = mm(inverse, sketch, NT)
        other = value[:, rank:]
        low_part = jnp.where(own_bit == 0, projected, other)
        high_part = jnp.where(own_bit == 0, other, projected)
        projected = mm(mixer, jnp.concatenate([low_part, high_part], axis=0))

    parts = split(mixer)

    @pl.loop(0, rows // WIDTH)
    def _(i):
        out = mm3(parts, split(wide(pairs, levels - 1, i * WIDTH)))
        for w in range(WIDTH):
            basis[i * WIDTH + w] = out[:, w * cells : (w + 1) * cells]

    cores[...] = projected * (1.0 / math.sqrt(rank))

    @pl.when(depth < depths - 1)
    def _():
        for c in halo_copies(0):
            c.wait_send()

    @pl.when(depth > 0)
    def _():
        for c in halo_copies(1):
            c.wait_send()


def body(probes, courant, sketches):
    depths = lax.axis_size("depth")
    levels = lax.axis_size("shot").bit_length() - 1
    local = jnp.transpose(probes[0], (1, 0, 2))
    rows, rank, cells = local.shape
    f32 = jnp.float32
    vmem = pl.BlockSpec(memory_space=pltpu.VMEM)
    dma = pltpu.SemaphoreType.DMA
    basis, cores = pl.pallas_call(
        functools.partial(kernel, depths, levels),
        out_shape=(
            jax.ShapeDtypeStruct((rows, rank, cells), f32),
            jax.ShapeDtypeStruct((rank, rank), f32),
        ),
        in_specs=[vmem] * 3,
        out_specs=(vmem, vmem),
        scratch_shapes=[
            pltpu.VMEM((2, STEPS, rank, cells), jnp.bfloat16),
            pltpu.VMEM((rows + 2 * STEPS, cells), f32),
            pltpu.VMEM((rows + 2 * STEPS, rank, cells), f32),
            pltpu.VMEM((rows + 2 * STEPS, rank, cells), f32),
            pltpu.VMEM((levels, rows, 2 * rank, cells), f32),
            pltpu.VMEM((levels, 2 * rank, 2 * rank), f32),
            pltpu.VMEM((levels, depths, 2 * rank, 2 * rank), f32),
            dma((2,)),
            dma((2,)),
            dma((2,)),
            dma((2,)),
            dma((levels, 2 ** (levels - 1), PIECES)),
            dma((levels, 2 ** (levels - 1), PIECES)),
            dma((levels, depths)),
            dma((levels, depths)),
        ],
        compiler_params=pltpu.CompilerParams(
            collective_id=0, has_side_effects=True, vmem_limit_bytes=56 * 2**20
        ),
    )(local, courant, sketches)
    return (jnp.transpose(basis, (1, 0, 2)), cores[None])


def choose(bit_value, low, high):
    return jnp.where(bit_value == 0, low, high)


def merged(sketch, near, theirs):
    half = mm(
        jnp.concatenate([0.5 * sketch, near], axis=1),
        jnp.concatenate([sketch, theirs], axis=1),
        NT,
    )
    return half + jnp.transpose(half)


def plane_kernel(
    depths,
    probes,
    speed,
    sketches,
    basis,
    cores,
    halo,
    wide_speed,
    field_a,
    field_b,
    pair,
    whole,
    first_sum,
    first_in,
    gram_all,
    quad_part,
    quad_in,
    quad_sum,
    quad_depth,
    quad_all,
    root_part,
    root_in,
    root_sum,
    root_depth,
    root_all,
    quad_mixer,
    quad_mixer_in,
    root_mixer,
    root_mixer_in,
    gathered,
    send_sems,
    recv_sems,
    local_sems,
):
    rows, rank, cells = probes.shape
    shots = 8
    per = rows // shots
    part = 2 * rank // 4
    shot = lax.axis_index("shot")
    depth = lax.axis_index("depth")

    def bit(h, of=shot):
        return lax.rem(of // (2**h), 2)

    def flip(mask, of=shot):
        value = 0
        for h in range(3):
            value += 2**h * (1 - bit(h, of) if mask >> h & 1 else bit(h, of))
        return value

    core, low_x, low_y = bit(0), bit(1), bit(2)

    barrier = pltpu.get_barrier_semaphore()
    for mask in range(1, shots):
        pl.semaphore_signal(barrier, inc=1, device_id=(flip(mask), depth), device_id_type=MESH)
    for j in range(1, depths):
        other = lax.rem(depth + j, depths)
        pl.semaphore_signal(barrier, inc=1, device_id=(shot, other), device_id_type=MESH)
    pl.semaphore_wait(barrier, shots - 1 + depths - 1)

    used = [0]

    def apart(work):
        @pl.loop(0, 1 + shot // shots)
        def _(_):
            work()

    def take(count):
        used[0] += count
        return used[0] - count

    def copy(src, dst, sem, to):
        return pltpu.make_async_remote_copy(
            src_ref=src,
            dst_ref=dst,
            send_sem=send_sems.at[sem],
            recv_sem=recv_sems.at[sem],
            device_id=to,
            device_id_type=MESH,
        )

    halo_sem, speed_sem = take(2), take(2)

    def halo_copies(side):
        to = depth + 1 if side == 0 else depth - 1
        rows_out = pl.ds(rows - STEPS, STEPS) if side == 0 else pl.ds(0, STEPS)
        at = 0 if side == 0 else STEPS + rows
        return (
            copy(probes.at[rows_out], halo.at[side], halo_sem + side, (shot, to)),
            copy(
                speed.at[rows_out],
                wide_speed.at[pl.ds(at, STEPS)],
                speed_sem + side,
                (shot, to),
            ),
        )

    @pl.when(depth < depths - 1)
    def _():
        for c in halo_copies(0):
            c.start()

    @pl.when(depth > 0)
    def _():
        for c in halo_copies(1):
            c.start()

    @pl.loop(0, rows, unroll=4)
    def _(d):
        field_a[STEPS + d] = probes[d].astype(jnp.float32)

    wide_speed[STEPS : STEPS + rows] = speed[...]

    @pl.when(depth > 0)
    def _():
        for c in halo_copies(0):
            c.wait_recv()
        field_a[0:STEPS] = halo[0].astype(jnp.float32)

    @pl.when(depth == 0)
    def _():
        field_a[0:STEPS] = jnp.zeros((STEPS, rank, cells), jnp.float32)
        wide_speed[0:STEPS] = jnp.zeros((STEPS, cells), jnp.float32)

    @pl.when(depth < depths - 1)
    def _():
        for c in halo_copies(1):
            c.wait_recv()
        field_a[STEPS + rows : 2 * STEPS + rows] = halo[1].astype(jnp.float32)

    @pl.when(depth == depths - 1)
    def _():
        field_a[STEPS + rows : 2 * STEPS + rows] = jnp.zeros((STEPS, rank, cells), jnp.float32)
        wide_speed[STEPS + rows : 2 * STEPS + rows] = jnp.zeros((STEPS, cells), jnp.float32)

    lane = lax.broadcasted_iota(jnp.int32, (rank, cells), 1)
    not_first = lane > 0
    not_last = lane < cells - 1
    mine = pl.ds(pl.multiple_of(core * rank, rank), rank)

    def update(d, source, older):
        u = source[d]
        left = jnp.where(not_first, pltpu.roll(u, 1, 1), 0.0)
        right = jnp.where(not_last, pltpu.roll(u, cells - 1, 1), 0.0)
        laplace = source[d + 1] + source[d - 1] + right + left - 4.0 * u
        return 2.0 * u - older + wide_speed[pl.ds(d, 1)] * laplace

    for step in range(STEPS - 1):
        source, target = (field_a, field_b) if step % 2 == 0 else (field_b, field_a)

        @pl.loop(step + 1, 2 * STEPS + rows - step - 1, unroll=2)
        def _(d):
            older = source[d] if step == 0 else target[d]
            target[d] = update(d, source, older)

    pair_sem, spread_sem = take(shots), take(shots)

    def pair_copy(i):
        at = pl.ds(i * per, per)
        return copy(pair.at[at, mine], pair.at[at, mine], pair_sem + i, (flip(1), depth))

    def spread_copy(to, mask):
        at = pl.ds(to * per, per)
        into = pl.ds(pl.multiple_of(shot * rank, rank), rank)
        return copy(pair.at[at, mine], whole.at[:, into], spread_sem + mask, (to, depth))

    source, target = (field_a, field_b) if (STEPS - 1) % 2 == 0 else (field_b, field_a)

    @pl.loop(0, shots)
    def _(i):
        for w in range(per):
            d = STEPS + i * per + w
            pair[i * per + w, mine] = update(d, source, target[d])
        pair_copy(i).start()

        @pl.when(i // 2 != shot // 2)
        def _():
            mask = 0
            for h in range(3):
                mask += 2**h * lax.rem(bit(h, i) + bit(h), 2)
            spread_copy(i, mask).start()

    group = WIDTH // per

    def gram_body(t, total):
        for i in range(group):
            pair_copy(t * group + i).wait_recv()
        at = t * WIDTH
        x = split(jnp.concatenate([pair[at + i] for i in range(WIDTH)], axis=1))
        return total + mm3(x, x, NT)

    zero = jnp.zeros((2 * rank, 2 * rank), jnp.float32)
    gram = lax.fori_loop(0, rows // WIDTH, gram_body, zero)

    def depth_start(source, into, sem):
        @apart
        def _():
            for j in range(1, depths):
                other = lax.rem(depth + j, depths)
                copy(source, into.at[depth], sem + j, (shot, other)).start()

    def depth_finish(source, into, sem, value):
        @apart
        def _():
            for j in range(1, depths):
                other = lax.rem(depth + j, depths)
                copy(source, into.at[depth], sem + j, (shot, other)).wait_recv()

        total = None
        for j in range(depths):
            one = jnp.where(depth == j, value, into[j])
            total = one if total is None else total + one
        return total

    for into in (first_in, quad_depth, root_depth):
        into[depth] = jnp.zeros(into.shape[1:], jnp.float32)

    first_sem, first_pair_sem = take(depths), take(1)
    half = choose(core, gram[:rank], gram[rank:])
    first_sum[...] = half
    depth_start(first_sum, first_in, first_sem)
    own_rows = pl.ds(pl.multiple_of(shot // 2 * 2 * rank, 2 * rank), 2 * rank)
    for w in range(per):
        whole[w, own_rows] = pair[shot * per + w]
    gram_all[mine] = depth_finish(first_sum, first_in, first_sem, half)
    first_pair = copy(gram_all.at[mine], gram_all.at[mine], first_pair_sem, (flip(1), depth))
    apart(first_pair.start)
    apart(first_pair.wait_recv)
    gram = gram_all[...]

    low = inverse_factor(gram[:rank, :rank])
    high = inverse_factor(gram[rank:, rank:])

    @apart
    def _():
        for mask in range(2, shots):
            spread_copy(flip(mask), mask).wait_recv()

    def cross(first, second, size):
        total = None
        for w in range(0, per, 2):
            x = split(jnp.concatenate([whole[w, first : first + size], whole[w + 1, first : first + size]], axis=1))
            y = split(jnp.concatenate([whole[w, second : second + size], whole[w + 1, second : second + size]], axis=1))
            one = mm3(x, y, NT)
            total = one if total is None else total + one
        return total

    quad_sem, quad_depth_sem, quad_all_sem = take(shots), take(depths), take(4)
    root_sem, root_depth_sem, root_all_sem = take(shots), take(depths), take(shots)
    tall = 2 * rank // 4
    for q in range(2):
        value = cross(4 * rank * q, 4 * rank * q + 2 * rank, 2 * rank)
        for i in range(4):
            quad_part[4 * q + i] = value[i * tall : (i + 1) * tall]

    def scatter(source, into, sem, mask):
        return copy(source.at[flip(mask)], into.at[mask], sem + mask, (flip(mask), depth))

    @apart
    def _():
        for mask in range(1, shots):
            scatter(quad_part, quad_in, quad_sem, mask).start()

    value = cross(0, 4 * rank, 4 * rank)
    for i in range(shots):
        root_part[i] = value[i * tall : (i + 1) * tall]
    @apart
    def _():
        for mask in range(1, shots):
            scatter(root_part, root_in, root_sem, mask).start()

    def scattered(source, into, sem):
        @apart
        def _():
            for mask in range(1, shots):
                scatter(source, into, sem, mask).wait_recv()

        total = source[shot]
        for mask in range(1, shots):
            total = total + into[mask]
        return total

    def piece_copy(ref, at, sem, mask):
        here = pl.ds(pl.multiple_of(at * tall, tall), tall)
        return copy(ref.at[here], ref.at[here], sem + mask, (flip(mask), depth))

    sketch = sketches[shot // 2 * 2]
    left = mm(sketch[:, :rank], low)
    right = mm(sketch[:, rank:], high)
    mixed = merged(sketch, mm(left, gram[:rank, rank:]), right)

    quad_own = scattered(quad_part, quad_in, quad_sem)
    quad_sum[...] = quad_own
    depth_start(quad_sum, quad_depth, quad_depth_sem)

    inverse = inverse_factor(mixed)
    sketch = sketches[shot // 4 * 4 + 1]
    carry = mm(choose(low_x, sketch[:, :rank], sketch[:, rank:]), inverse)
    mine_quad = mm(carry, jnp.concatenate([left, right], axis=1))
    quad_mixer[...] = mine_quad
    exchange_sem = take(2)
    quad_exchange = copy(quad_mixer, quad_mixer_in, exchange_sem, (flip(2), depth))
    apart(quad_exchange.start)

    quad_at = 2 * low_x + core
    quad_all[pl.ds(pl.multiple_of(quad_at * tall, tall), tall)] = depth_finish(
        quad_sum, quad_depth, quad_depth_sem, quad_own
    )
    @apart
    def _():
        for mask in range(1, 4):
            piece_copy(quad_all, quad_at, quad_all_sem, mask).start()

    root_own = scattered(root_part, root_in, root_sem)
    root_sum[...] = root_own
    depth_start(root_sum, root_depth, root_depth_sem)
    @apart
    def _():
        for mask in range(1, 4):
            piece_copy(quad_all, quad_at, quad_all_sem, mask).wait_recv()

    quad = quad_all[...]
    near = choose(low_x, mm(mine_quad, quad), mm(mine_quad, quad, NT))
    apart(quad_exchange.wait_recv)
    their_quad = quad_mixer_in[...]
    mixed = merged(sketch, near, their_quad)

    root_all[pl.ds(pl.multiple_of(shot * tall, tall), tall)] = depth_finish(
        root_sum, root_depth, root_depth_sem, root_own
    )
    @apart
    def _():
        for mask in range(1, shots):
            piece_copy(root_all, shot, root_all_sem, mask).start()

    inverse = inverse_factor(mixed)
    sketch = sketches[3]
    carry = mm(choose(low_y, sketch[:, :rank], sketch[:, rank:]), inverse)
    joined = jnp.concatenate(
        [
            choose(low_x, mine_quad, their_quad),
            choose(low_x, their_quad, mine_quad),
        ],
        axis=1,
    )
    mine_root = mm(carry, joined)
    root_mixer[...] = mine_root
    root_exchange = copy(root_mixer, root_mixer_in, exchange_sem + 1, (flip(4), depth))
    apart(root_exchange.start)

    @apart
    def _():
        for mask in range(1, shots):
            piece_copy(root_all, shot, root_all_sem, mask).wait_recv()

    root = root_all[...]
    near = choose(low_y, mm(mine_root, root), mm(mine_root, root, NT))
    apart(root_exchange.wait_recv)
    their_root = root_mixer_in[...]
    inverse = inverse_factor(merged(sketch, near, their_root))
    mine_root = mm(inverse, mine_root)
    their_root = mm(inverse, their_root)
    mixer = jnp.concatenate(
        [
            choose(low_y, mine_root, their_root),
            choose(low_y, their_root, mine_root),
        ],
        axis=1,
    )

    share_sem = take(2 * shots)
    parts = split(mixer)

    def share_copy(mask, i):
        at = pl.ds(shot * per + 2 * i, 2)
        return copy(gathered.at[at], gathered.at[at], share_sem + 2 * mask + i, (flip(mask), depth))

    def forward_copy(mask, i):
        at = pl.ds(flip(mask) * per + 2 * i, 2)
        return copy(gathered.at[at], gathered.at[at], share_sem + 2 * (mask + 1) + i, (flip(1), depth))

    for i in range(per // 2):
        out = mm3(parts, split(jnp.concatenate([whole[2 * i], whole[2 * i + 1]], axis=1)))
        for w in range(2):
            gathered[shot * per + 2 * i + w] = out[:, w * cells : (w + 1) * cells]

        @apart
        def _():
            for mask in (6, 2, 4, 1):
                share_copy(mask, i).start()

    own = choose(low_x, mine_root[:, : 2 * rank], mine_root[:, 2 * rank :])
    other = choose(low_x, mine_root[:, 2 * rank :], mine_root[:, : 2 * rank])
    near = mm(own, gram)
    near += choose(low_x, mm(other, quad, NT), mm(other, quad))
    far = choose(low_y, mm(their_root, root, NT), mm(their_root, root))
    near += choose(low_x, far[:, : 2 * rank], far[:, 2 * rank :])
    cores[...] = choose(core, near[:, :rank], near[:, rank:]) * (1.0 / math.sqrt(rank))

    @apart
    def _():
        for i in range(per // 2):
            for mask in (2, 4, 6):
                share_copy(mask, i).wait_recv()
                forward_copy(mask, i).start()
        for i in range(per // 2):
            for mask in (1, 3, 5, 7):
                share_copy(mask, i).wait_recv()

    out_copy = pltpu.make_async_copy(gathered, basis, local_sems.at[0])
    out_copy.start()

    @pl.when(depth < depths - 1)
    def _():
        for c in halo_copies(0):
            c.wait_send()

    @pl.when(depth > 0)
    def _():
        for c in halo_copies(1):
            c.wait_send()

    for i in range(shots):
        pair_copy(i).wait_send()
    for mask in range(2, shots):
        spread_copy(flip(mask), mask).wait_send()
    for source, into, sem in (
        (first_sum, first_in, first_sem),
        (quad_sum, quad_depth, quad_depth_sem),
        (root_sum, root_depth, root_depth_sem),
    ):
        for j in range(1, depths):
            other = lax.rem(depth + j, depths)
            copy(source, into.at[depth], sem + j, (shot, other)).wait_send()
    first_pair.wait_send()
    for mask in range(1, shots):
        scatter(quad_part, quad_in, quad_sem, mask).wait_send()
        scatter(root_part, root_in, root_sem, mask).wait_send()
        piece_copy(root_all, shot, root_all_sem, mask).wait_send()
    for mask in range(1, 4):
        piece_copy(quad_all, quad_at, quad_all_sem, mask).wait_send()
    quad_exchange.wait_send()
    root_exchange.wait_send()
    for i in range(per // 2):
        for mask in (1, 2, 4, 6):
            share_copy(mask, i).wait_send()
        for mask in (2, 4, 6):
            forward_copy(mask, i).wait_send()
    out_copy.wait()
    assert used[0] <= SEMS


SEMS = 112


def plane_body(probes, courant, sketches):
    depths = lax.axis_size("depth")
    shots = lax.axis_size("shot")
    local = jnp.transpose(probes[0], (1, 0, 2))
    rows, rank, cells = local.shape
    per = rows // shots
    tall = rank // 2
    f32 = jnp.float32
    vmem = pl.BlockSpec(memory_space=pltpu.VMEM)
    dma = pltpu.SemaphoreType.DMA

    def scratch(*shape):
        return pltpu.VMEM(shape, f32)

    basis, cores = pl.pallas_call(
        functools.partial(plane_kernel, depths),
        out_shape=(
            jax.ShapeDtypeStruct((rows, rank, cells), f32),
            jax.ShapeDtypeStruct((rank, rank), f32),
        ),
        in_specs=[vmem] * 3,
        out_specs=(pl.BlockSpec(memory_space=pl.ANY), vmem),
        scratch_shapes=[
            pltpu.VMEM((2, STEPS, rank, cells), jnp.bfloat16),
            scratch(rows + 2 * STEPS, cells),
            scratch(rows + 2 * STEPS, rank, cells),
            scratch(rows + 2 * STEPS, rank, cells),
            scratch(rows, 2 * rank, cells),
            scratch(per, shots * rank, cells),
            scratch(rank, 2 * rank),
            scratch(depths, rank, 2 * rank),
            scratch(2 * rank, 2 * rank),
            scratch(shots, tall, 2 * rank),
            scratch(shots, tall, 2 * rank),
            scratch(tall, 2 * rank),
            scratch(depths, tall, 2 * rank),
            scratch(2 * rank, 2 * rank),
            scratch(shots, tall, 4 * rank),
            scratch(shots, tall, 4 * rank),
            scratch(tall, 4 * rank),
            scratch(depths, tall, 4 * rank),
            scratch(4 * rank, 4 * rank),
            scratch(rank, 2 * rank),
            scratch(rank, 2 * rank),
            scratch(rank, 4 * rank),
            scratch(rank, 4 * rank),
            scratch(rows, rank, cells),
            dma((SEMS,)),
            dma((SEMS,)),
            dma((1,)),
        ],
        compiler_params=pltpu.CompilerParams(
            collective_id=0, has_side_effects=True, vmem_limit_bytes=56 * 2**20
        ),
    )(local, courant, jnp.transpose(sketches, (0, 2, 1)))
    return (jnp.transpose(basis, (1, 0, 2)), cores[None])


def solution(mesh):
    placed = (P("shot", None, "depth", None), P("depth", None), P())
    plane = mesh.shape["shot"] == 8
    return jax.shard_map(
        plane_body if plane else body,
        mesh=mesh,
        in_specs=placed,
        out_specs=(P(None, "depth", None), P("shot", None, None)),
        check_vma=False,
    )
```

```python
import functools
import math

import jax
import jax.numpy as jnp
from jax import lax
from jax.experimental import pallas as pl
from jax.experimental.pallas import tpu as pltpu
from jax.sharding import PartitionSpec as P

STEPS = 4
MESH = pl.DeviceIdType.MESH
HI = lax.Precision.HIGHEST
NN = (((1,), (0,)), ((), ()))
NT = (((1,), (1,)), ((), ()))
TN = (((0,), (0,)), ((), ()))
PIECES = 2
WIDTH = 8


def mm(a, b, dims=NN):
    return lax.dot_general(a, b, dims, precision=HI, preferred_element_type=jnp.float32)


def split(x):
    top = x.astype(jnp.bfloat16)
    return top, (x - top.astype(jnp.float32)).astype(jnp.bfloat16)


def mm3(a, b, dims=NN):
    def part(p, q):
        return lax.dot_general(p, q, dims, preferred_element_type=jnp.float32)

    return part(a[0], b[0]) + (part(a[0], b[1]) + part(a[1], b[0]))


def wide(ref, h, d, picked=slice(None)):
    return jnp.concatenate([ref[h, d + i, picked] for i in range(WIDTH)], axis=1)


def inverse_factor(gram):
    n = gram.shape[0]
    rows = lax.broadcasted_iota(jnp.int32, (n, 1), 0)
    eye = (
        lax.broadcasted_iota(jnp.int32, (n, n), 0) == lax.broadcasted_iota(jnp.int32, (n, n), 1)
    ).astype(jnp.float32)
    a = jnp.concatenate([gram, eye], axis=1)
    blocks = [a[8 * b : 8 * b + 8] for b in range(n // 8)]
    for k in range(0, n, 2):
        b0, r = divmod(k, 8)
        first, second = blocks[b0][r : r + 1], blocks[b0][r + 1 : r + 2]
        p, q, s = first[:, k : k + 1], second[:, k : k + 1], second[:, k + 1 : k + 2]
        if k == n - 2:
            break
        scale = 1.0 / (p * s - q * q)
        row0 = (s * first - q * second) * scale
        row1 = (p * second - q * first) * scale
        for b in range((k + 2) // 8, n // 8):
            col0, col1 = blocks[b][:, k : k + 1], blocks[b][:, k + 1 : k + 2]
            if b == b0:
                below = rows[:8] > r + 1
                col0, col1 = jnp.where(below, col0, 0.0), jnp.where(below, col1, 0.0)
            blocks[b] = blocks[b] - (col0 * row0 + col1 * row1)
    a = jnp.concatenate(blocks, axis=0)
    before = jnp.concatenate([a[n - 1 :], a[: n - 1]], axis=0)
    even = lax.rem(rows, 2) == 0
    own = jnp.sum(a[:, :n] * eye, axis=1, keepdims=True)
    shifted = jnp.concatenate([eye[n - 1 :], eye[: n - 1]], axis=0)
    side = jnp.sum(a[:, :n] * shifted, axis=1, keepdims=True)
    above = jnp.sum(before[:, :n] * shifted, axis=1, keepdims=True)
    ratio = jnp.where(even, 0.0, side / jnp.where(even, 1.0, above))
    value = own - ratio * side
    return (a[:, n:] - ratio * before[:, n:]) * (1.0 / jnp.sqrt(value))


def kernel(
    depths,
    levels,
    probes,
    speed,
    sketches,
    basis,
    cores,
    halo,
    wide_speed,
    field_a,
    field_b,
    pairs,
    sums,
    sums_in,
    halo_send,
    halo_recv,
    speed_send,
    speed_recv,
    pair_send,
    pair_recv,
    sum_send,
    sum_recv,
):
    rows, rank, cells = probes.shape
    shot = lax.axis_index("shot")
    depth = lax.axis_index("depth")
    low_end = depth == 0
    high_end = depth == depths - 1

    def bit(h):
        return lax.rem(shot // (2**h), 2)

    def peer(h):
        return shot + 2**h - 2 ** (h + 1) * bit(h)

    barrier = pltpu.get_barrier_semaphore()
    for h in range(levels):
        pl.semaphore_signal(barrier, inc=1, device_id=(peer(h), depth), device_id_type=MESH)
    for j in range(1, depths):
        other = lax.rem(depth + j, depths)
        pl.semaphore_signal(barrier, inc=1, device_id=(shot, other), device_id_type=MESH)
    pl.semaphore_wait(barrier, levels + depths - 1)

    def halo_copies(side):
        to = depth + 1 if side == 0 else depth - 1
        rows_out = pl.ds(rows - STEPS, STEPS) if side == 0 else pl.ds(0, STEPS)
        first = pltpu.make_async_remote_copy(
            src_ref=probes.at[rows_out],
            dst_ref=halo.at[side],
            send_sem=halo_send.at[side],
            recv_sem=halo_recv.at[side],
            device_id=(shot, to),
            device_id_type=MESH,
        )
        at = 0 if side == 0 else STEPS + rows
        second = pltpu.make_async_remote_copy(
            src_ref=speed.at[rows_out],
            dst_ref=wide_speed.at[pl.ds(at, STEPS)],
            send_sem=speed_send.at[side],
            recv_sem=speed_recv.at[side],
            device_id=(shot, to),
            device_id_type=MESH,
        )
        return first, second

    @pl.when(depth < depths - 1)
    def _():
        for c in halo_copies(0):
            c.start()

    @pl.when(depth > 0)
    def _():
        for c in halo_copies(1):
            c.start()

    @pl.loop(0, rows, unroll=4)
    def _(d):
        field_a[STEPS + d] = probes[d].astype(jnp.float32)

    wide_speed[STEPS : STEPS + rows] = speed[...]

    @pl.when(depth > 0)
    def _():
        for c in halo_copies(0):
            c.wait_recv()
        field_a[0:STEPS] = halo[0].astype(jnp.float32)

    @pl.when(depth == 0)
    def _():
        field_a[0:STEPS] = jnp.zeros((STEPS, rank, cells), jnp.float32)
        wide_speed[0:STEPS] = jnp.zeros((STEPS, cells), jnp.float32)

    @pl.when(depth < depths - 1)
    def _():
        for c in halo_copies(1):
            c.wait_recv()
        field_a[STEPS + rows : 2 * STEPS + rows] = halo[1].astype(jnp.float32)

    @pl.when(depth == depths - 1)
    def _():
        field_a[STEPS + rows : 2 * STEPS + rows] = jnp.zeros((STEPS, rank, cells), jnp.float32)
        wide_speed[STEPS + rows : 2 * STEPS + rows] = jnp.zeros((STEPS, cells), jnp.float32)

    lane = lax.broadcasted_iota(jnp.int32, (rank, cells), 1)
    not_first = lane > 0
    not_last = lane < cells - 1
    me = bit(0)
    mine = pl.ds(pl.multiple_of(me * rank, rank), rank)

    def update(d, source, older):
        u = source[d]
        left = jnp.where(not_first, pltpu.roll(u, 1, 1), 0.0)
        right = jnp.where(not_last, pltpu.roll(u, cells - 1, 1), 0.0)
        laplace = source[d + 1] + source[d - 1] + right + left - 4.0 * u
        return 2.0 * u - older + wide_speed[pl.ds(d, 1)] * laplace

    for step in range(STEPS):
        source, target = (field_a, field_b) if step % 2 == 0 else (field_b, field_a)
        last = step == STEPS - 1

        @pl.loop(step + 1, 2 * STEPS + rows - step - 1, unroll=2)
        def _(d):
            older = source[d] if step == 0 else target[d]
            new = update(d, source, older)
            if last:
                pairs[0, d - STEPS, mine] = new
            else:
                target[d] = new

    def pair_copy(h):
        own = pl.ds(pl.multiple_of(bit(h) * rank, rank), rank)
        return [
            pltpu.make_async_remote_copy(
                src_ref=pairs.at[h, :, own],
                dst_ref=pairs.at[h, :, own],
                send_sem=pair_send.at[h, 0, 0],
                recv_sem=pair_recv.at[h, 0, 0],
                device_id=(peer(h), depth),
                device_id_type=MESH,
            )
        ]

    for c in pair_copy(0):
        c.start()
    for c in pair_copy(0):
        c.wait()

    def gram_body(d, total):
        x = split(wide(pairs, 0, d * WIDTH))
        return total + mm3(x, x, NT)

    zero = jnp.zeros((2 * rank, 2 * rank), jnp.float32)
    gram = lax.fori_loop(0, rows // WIDTH, gram_body, zero)

    def sum_copy(h, j):
        other = lax.rem(depth + j, depths)
        size = 2 * rank if h == 0 else rank
        return pltpu.make_async_remote_copy(
            src_ref=sums.at[h, pl.ds(0, size)],
            dst_ref=sums_in.at[h, depth, pl.ds(0, size)],
            send_sem=sum_send.at[h, j],
            recv_sem=sum_recv.at[h, j],
            device_id=(shot, other),
            device_id_type=MESH,
        )

    def depth_sum(h, value):
        size = value.shape[0]
        sums[h, 0:size] = value
        for j in range(1, depths):
            sum_copy(h, j).start()
        for j in range(1, depths):
            sum_copy(h, j).wait()
        total = None
        for j in range(depths):
            part = jnp.where(depth == j, value, sums_in[h, j, 0:size])
            total = part if total is None else total + part
        return total

    for h in range(levels):
        sums_in[h, depth] = jnp.zeros((2 * rank, 2 * rank), jnp.float32)
    gram = depth_sum(0, gram)

    low = inverse_factor(gram[:rank, :rank])
    high = inverse_factor(gram[rank:, rank:])
    sketch = sketches[shot // 2 * 2]
    mixer = jnp.concatenate(
        [mm(sketch[:rank], low, TN), mm(sketch[rank:], high, TN)], axis=1
    )
    carried = mm(mixer, gram)
    inverse = inverse_factor(mm(carried, mixer, NT))
    mixer = mm(inverse, mixer)
    carried = mm(inverse, carried)
    projected = jnp.where(me == 0, carried[:, :rank], carried[:, rank:])

    for h in range(1, levels):
        own_bit = bit(h)
        own = pl.ds(pl.multiple_of(own_bit * rank, rank), rank)

        parts = split(mixer)
        part_rows = rows // 2**h
        per = part_rows // PIECES
        got = pl.ds(pl.multiple_of((1 - own_bit) * rank, rank), rank)

        def part_at(mask, i):
            part = 0
            for b in range(h):
                part += 2**b * (1 - bit(b) if mask >> b & 1 else bit(b))
            return pl.ds(part * part_rows + i * per, per)

        def part_copy(mask, i):
            low = mask & -mask
            at = part_at(mask - low, i)
            lanes = got if mask else own
            return pltpu.make_async_remote_copy(
                src_ref=pairs.at[h, at, lanes],
                dst_ref=pairs.at[h, at, lanes],
                send_sem=pair_send.at[h, mask, i],
                recv_sem=pair_recv.at[h, mask, i],
                device_id=(peer(low.bit_length() - 1 if mask else h), depth),
                device_id_type=MESH,
            )

        chunks = rows // WIDTH
        ahead = max(1, part_rows // WIDTH)
        first = part_at(0, 0).start // WIDTH
        for t in range(chunks):
            at = lax.rem(first + t, chunks) * WIDTH
            out = mm3(parts, split(wide(pairs, h - 1, at)))
            for w in range(WIDTH):
                pairs[h, at + w, own] = out[:, w * cells : (w + 1) * cells]
            if per == WIDTH and t < PIECES:
                part_copy(0, t).start()
            elif per != WIDTH and t == ahead - 1:
                for i in range(PIECES):
                    part_copy(0, i).start()
        masks = sorted(range(2**h), key=lambda m: (m.bit_count(), -m))
        for mask in masks:
            low = mask & -mask if mask else 2**h
            for i in range(PIECES):
                part_copy(mask, i).wait_recv()
                for b in reversed(range(low.bit_length() - 1)):
                    part_copy(mask + 2**b, i).start()
        for mask in masks:
            for i in range(PIECES):
                part_copy(mask, i).wait_send()

        def cross_body(d, total):
            y = split(wide(pairs, h, d * WIDTH))
            r = split(wide(pairs, 0, d * WIDTH, mine))
            right = [jnp.concatenate([p[rank:], q], axis=0) for p, q in zip(y, r)]
            return total + mm3(y, right, NT)

        cross = lax.fori_loop(0, rows // WIDTH, cross_body, zero)
        value = jnp.concatenate(
            [
                cross[:rank, :rank],
                jnp.where(own_bit == 0, cross[rank:, rank:], cross[:rank, rank:]),
            ],
            axis=1,
        )
        value = depth_sum(h, value)
        stride = 2**h
        sketch = sketches[shot // (2 * stride) * (2 * stride) + stride - 1]
        top, bottom = sketch[:rank], sketch[rank:]
        across = value[:, :rank]
        mixed = mm(sketch, sketch, TN)
        mixed += mm(top, mm(across, bottom), TN) + mm(bottom, mm(across, top, TN), TN)
        inverse = inverse_factor(mixed)
        mixer = mm(inverse, sketch, NT)
        other = value[:, rank:]
        low_part = jnp.where(own_bit == 0, projected, other)
        high_part = jnp.where(own_bit == 0, other, projected)
        projected = mm(mixer, jnp.concatenate([low_part, high_part], axis=0))

    parts = split(mixer)

    @pl.loop(0, rows // WIDTH)
    def _(i):
        out = mm3(parts, split(wide(pairs, levels - 1, i * WIDTH)))
        for w in range(WIDTH):
            basis[i * WIDTH + w] = out[:, w * cells : (w + 1) * cells]

    cores[...] = projected * (1.0 / math.sqrt(rank))

    @pl.when(depth < depths - 1)
    def _():
        for c in halo_copies(0):
            c.wait_send()

    @pl.when(depth > 0)
    def _():
        for c in halo_copies(1):
            c.wait_send()


def body(probes, courant, sketches):
    depths = lax.axis_size("depth")
    levels = lax.axis_size("shot").bit_length() - 1
    local = jnp.transpose(probes[0], (1, 0, 2))
    rows, rank, cells = local.shape
    f32 = jnp.float32
    vmem = pl.BlockSpec(memory_space=pltpu.VMEM)
    dma = pltpu.SemaphoreType.DMA
    basis, cores = pl.pallas_call(
        functools.partial(kernel, depths, levels),
        out_shape=(
            jax.ShapeDtypeStruct((rows, rank, cells), f32),
            jax.ShapeDtypeStruct((rank, rank), f32),
        ),
        in_specs=[vmem] * 3,
        out_specs=(vmem, vmem),
        scratch_shapes=[
            pltpu.VMEM((2, STEPS, rank, cells), jnp.bfloat16),
            pltpu.VMEM((rows + 2 * STEPS, cells), f32),
            pltpu.VMEM((rows + 2 * STEPS, rank, cells), f32),
            pltpu.VMEM((rows + 2 * STEPS, rank, cells), f32),
            pltpu.VMEM((levels, rows, 2 * rank, cells), f32),
            pltpu.VMEM((levels, 2 * rank, 2 * rank), f32),
            pltpu.VMEM((levels, depths, 2 * rank, 2 * rank), f32),
            dma((2,)),
            dma((2,)),
            dma((2,)),
            dma((2,)),
            dma((levels, 2 ** (levels - 1), PIECES)),
            dma((levels, 2 ** (levels - 1), PIECES)),
            dma((levels, depths)),
            dma((levels, depths)),
        ],
        compiler_params=pltpu.CompilerParams(
            collective_id=0, has_side_effects=True, vmem_limit_bytes=56 * 2**20
        ),
    )(local, courant, sketches)
    return (jnp.transpose(basis, (1, 0, 2)), cores[None])


def choose(bit_value, low, high):
    return jnp.where(bit_value == 0, low, high)


def merged(sketch, near, theirs):
    half = mm(
        jnp.concatenate([0.5 * sketch, near], axis=1),
        jnp.concatenate([sketch, theirs], axis=1),
        NT,
    )
    return half + jnp.transpose(half)


def plane_kernel(
    depths,
    probes_in,
    speed_in,
    sketches_in,
    basis,
    cores,
    probes,
    speed,
    sketches,
    flat,
    edges,
    halo,
    wide_speed,
    field_a,
    field_b,
    pair,
    whole,
    first_sum,
    first_in,
    gram_all,
    quad_part,
    quad_in,
    quad_sum,
    quad_depth,
    quad_all,
    root_part,
    root_in,
    root_sum,
    root_depth,
    root_all,
    quad_mixer,
    quad_mixer_in,
    root_mixer,
    root_mixer_in,
    gathered,
    send_sems,
    recv_sems,
    local_sems,
):
    rank, rows, cells = probes.shape
    shots = 8
    per = rows // shots
    part = 2 * rank // 4
    shot = lax.axis_index("shot")
    depth = lax.axis_index("depth")

    def bit(h, of=shot):
        return lax.rem(of // (2**h), 2)

    def flip(mask, of=shot):
        value = 0
        for h in range(3):
            value += 2**h * (1 - bit(h, of) if mask >> h & 1 else bit(h, of))
        return value

    core, low_x, low_y = bit(0), bit(1), bit(2)

    barrier = pltpu.get_barrier_semaphore()
    for mask in range(1, shots):
        pl.semaphore_signal(barrier, inc=1, device_id=(flip(mask), depth), device_id_type=MESH)
    for j in range(1, depths):
        other = lax.rem(depth + j, depths)
        pl.semaphore_signal(barrier, inc=1, device_id=(shot, other), device_id_type=MESH)

    loads = [
        pltpu.make_async_copy(probes_in, probes, local_sems.at[rows]),
        pltpu.make_async_copy(speed_in, speed, local_sems.at[rows + 1]),
        pltpu.make_async_copy(sketches_in, sketches, local_sems.at[rows + 2]),
    ]
    for c in loads:
        c.start()
    loads[0].wait()

    @pl.loop(0, rank, unroll=4)
    def _(i):
        at = pl.ds(pl.multiple_of(i * rows, rows), rows)
        flat[at] = probes[i].astype(jnp.float32)

    @pl.loop(0, rows, unroll=4)
    def _(d):
        field_a[STEPS + d] = flat[pl.ds(d, rank, stride=rows)]

    for d in range(STEPS):
        edges[0, d] = field_a[rows + d].astype(jnp.bfloat16)
        edges[1, d] = field_a[STEPS + d].astype(jnp.bfloat16)
    loads[1].wait()
    wide_speed[STEPS : STEPS + rows] = speed[...]

    @pl.loop(0, 1 + shot // shots)
    def _(_):
        pl.semaphore_wait(barrier, shots - 1 + depths - 1)

    used = [0]

    def apart(work):
        @pl.loop(0, 1 + shot // shots)
        def _(_):
            work()

    def take(count):
        used[0] += count
        return used[0] - count

    def copy(src, dst, sem, to):
        return pltpu.make_async_remote_copy(
            src_ref=src,
            dst_ref=dst,
            send_sem=send_sems.at[sem],
            recv_sem=recv_sems.at[sem],
            device_id=to,
            device_id_type=MESH,
        )

    halo_sem, speed_sem = take(2), take(2)

    def halo_copies(side):
        to = depth + 1 if side == 0 else depth - 1
        rows_out = pl.ds(rows - STEPS, STEPS) if side == 0 else pl.ds(0, STEPS)
        at = 0 if side == 0 else STEPS + rows
        return (
            copy(edges.at[side], halo.at[side], halo_sem + side, (shot, to)),
            copy(
                speed.at[rows_out],
                wide_speed.at[pl.ds(at, STEPS)],
                speed_sem + side,
                (shot, to),
            ),
        )

    @pl.when(depth < depths - 1)
    def _():
        for c in halo_copies(0):
            c.start()

    @pl.when(depth > 0)
    def _():
        for c in halo_copies(1):
            c.start()

    @pl.when(depth > 0)
    def _():
        for c in halo_copies(0):
            c.wait_recv()
        field_a[0:STEPS] = halo[0].astype(jnp.float32)

    @pl.when(depth == 0)
    def _():
        field_a[0:STEPS] = jnp.zeros((STEPS, rank, cells), jnp.float32)
        wide_speed[0:STEPS] = jnp.zeros((STEPS, cells), jnp.float32)

    @pl.when(depth < depths - 1)
    def _():
        for c in halo_copies(1):
            c.wait_recv()
        field_a[STEPS + rows : 2 * STEPS + rows] = halo[1].astype(jnp.float32)

    @pl.when(depth == depths - 1)
    def _():
        field_a[STEPS + rows : 2 * STEPS + rows] = jnp.zeros((STEPS, rank, cells), jnp.float32)
        wide_speed[STEPS + rows : 2 * STEPS + rows] = jnp.zeros((STEPS, cells), jnp.float32)

    lane = lax.broadcasted_iota(jnp.int32, (rank, cells), 1)
    not_first = lane > 0
    not_last = lane < cells - 1
    mine = pl.ds(pl.multiple_of(core * rank, rank), rank)

    def update(d, source, older):
        u = source[d]
        left = jnp.where(not_first, pltpu.roll(u, 1, 1), 0.0)
        right = jnp.where(not_last, pltpu.roll(u, cells - 1, 1), 0.0)
        laplace = source[d + 1] + source[d - 1] + right + left - 4.0 * u
        return 2.0 * u - older + wide_speed[pl.ds(d, 1)] * laplace

    for step in range(STEPS - 1):
        source, target = (field_a, field_b) if step % 2 == 0 else (field_b, field_a)

        @pl.loop(step + 1, 2 * STEPS + rows - step - 1, unroll=2)
        def _(d):
            older = source[d] if step == 0 else target[d]
            target[d] = update(d, source, older)

    pair_sem, spread_sem = take(shots), take(shots)

    def pair_copy(i):
        at = pl.ds(i * per, per)
        return copy(pair.at[at, mine], pair.at[at, mine], pair_sem + i, (flip(1), depth))

    def spread_copy(to, mask):
        at = pl.ds(to * per, per)
        into = pl.ds(pl.multiple_of(shot * rank, rank), rank)
        return copy(pair.at[at, mine], whole.at[:, into], spread_sem + mask, (to, depth))

    source, target = (field_a, field_b) if (STEPS - 1) % 2 == 0 else (field_b, field_a)

    @pl.loop(0, shots)
    def _(i):
        for w in range(per):
            d = STEPS + i * per + w
            pair[i * per + w, mine] = update(d, source, target[d])
        pair_copy(i).start()

        @pl.when(i // 2 != shot // 2)
        def _():
            mask = 0
            for h in range(3):
                mask += 2**h * lax.rem(bit(h, i) + bit(h), 2)
            spread_copy(i, mask).start()

    group = WIDTH // per

    def gram_body(t, total):
        for i in range(group):
            pair_copy(t * group + i).wait_recv()
        at = t * WIDTH
        x = split(jnp.concatenate([pair[at + i] for i in range(WIDTH)], axis=1))
        return total + mm3(x, x, NT)

    zero = jnp.zeros((2 * rank, 2 * rank), jnp.float32)
    gram = lax.fori_loop(0, rows // WIDTH, gram_body, zero)

    def depth_start(source, into, sem):
        @apart
        def _():
            for j in range(1, depths):
                other = lax.rem(depth + j, depths)
                copy(source, into.at[depth], sem + j, (shot, other)).start()

    def depth_finish(source, into, sem, value):
        @apart
        def _():
            for j in range(1, depths):
                other = lax.rem(depth + j, depths)
                copy(source, into.at[depth], sem + j, (shot, other)).wait_recv()

        total = None
        for j in range(depths):
            one = jnp.where(depth == j, value, into[j])
            total = one if total is None else total + one
        return total

    for into in (first_in, quad_depth, root_depth):
        into[depth] = jnp.zeros(into.shape[1:], jnp.float32)

    first_sem, first_pair_sem = take(depths), take(1)
    half = choose(core, gram[:rank], gram[rank:])
    first_sum[...] = half
    depth_start(first_sum, first_in, first_sem)
    own_rows = pl.ds(pl.multiple_of(shot // 2 * 2 * rank, 2 * rank), 2 * rank)
    for w in range(per):
        whole[w, own_rows] = pair[shot * per + w]
    gram_all[mine] = depth_finish(first_sum, first_in, first_sem, half)
    first_pair = copy(gram_all.at[mine], gram_all.at[mine], first_pair_sem, (flip(1), depth))
    apart(first_pair.start)
    apart(first_pair.wait_recv)
    gram = gram_all[...]

    loads[2].wait()
    low = inverse_factor(gram[:rank, :rank])
    high = inverse_factor(gram[rank:, rank:])

    @apart
    def _():
        for mask in range(2, shots):
            spread_copy(flip(mask), mask).wait_recv()

    def cross(first, second, size):
        total = None
        for w in range(0, per, 2):
            x = split(jnp.concatenate([whole[w, first : first + size], whole[w + 1, first : first + size]], axis=1))
            y = split(jnp.concatenate([whole[w, second : second + size], whole[w + 1, second : second + size]], axis=1))
            one = mm3(x, y, NT)
            total = one if total is None else total + one
        return total

    quad_sem, quad_depth_sem, quad_all_sem = take(shots), take(depths), take(4)
    root_sem, root_depth_sem, root_all_sem = take(shots), take(depths), take(shots)
    tall = 2 * rank // 4
    for q in range(2):
        value = cross(4 * rank * q, 4 * rank * q + 2 * rank, 2 * rank)
        for i in range(4):
            quad_part[4 * q + i] = value[i * tall : (i + 1) * tall]

    def scatter(source, into, sem, mask):
        return copy(source.at[flip(mask)], into.at[mask], sem + mask, (flip(mask), depth))

    @apart
    def _():
        for mask in range(1, shots):
            scatter(quad_part, quad_in, quad_sem, mask).start()

    value = cross(0, 4 * rank, 4 * rank)
    for i in range(shots):
        root_part[i] = value[i * tall : (i + 1) * tall]
    @apart
    def _():
        for mask in range(1, shots):
            scatter(root_part, root_in, root_sem, mask).start()

    def scattered(source, into, sem):
        @apart
        def _():
            for mask in range(1, shots):
                scatter(source, into, sem, mask).wait_recv()

        total = source[shot]
        for mask in range(1, shots):
            total = total + into[mask]
        return total

    def piece_copy(ref, at, sem, mask):
        here = pl.ds(pl.multiple_of(at * tall, tall), tall)
        return copy(ref.at[here], ref.at[here], sem + mask, (flip(mask), depth))

    sketch = sketches[shot // 2 * 2]
    left = mm(sketch[:, :rank], low)
    right = mm(sketch[:, rank:], high)
    mixed = merged(sketch, mm(left, gram[:rank, rank:]), right)

    quad_own = scattered(quad_part, quad_in, quad_sem)
    quad_sum[...] = quad_own
    depth_start(quad_sum, quad_depth, quad_depth_sem)

    inverse = inverse_factor(mixed)
    sketch = sketches[shot // 4 * 4 + 1]
    carry = mm(choose(low_x, sketch[:, :rank], sketch[:, rank:]), inverse)
    mine_quad = mm(carry, jnp.concatenate([left, right], axis=1))
    quad_mixer[...] = mine_quad
    exchange_sem = take(2)
    quad_exchange = copy(quad_mixer, quad_mixer_in, exchange_sem, (flip(2), depth))
    apart(quad_exchange.start)

    quad_at = 2 * low_x + core
    quad_all[pl.ds(pl.multiple_of(quad_at * tall, tall), tall)] = depth_finish(
        quad_sum, quad_depth, quad_depth_sem, quad_own
    )
    @apart
    def _():
        for mask in range(1, 4):
            piece_copy(quad_all, quad_at, quad_all_sem, mask).start()

    root_own = scattered(root_part, root_in, root_sem)
    root_sum[...] = root_own
    depth_start(root_sum, root_depth, root_depth_sem)
    @apart
    def _():
        for mask in range(1, 4):
            piece_copy(quad_all, quad_at, quad_all_sem, mask).wait_recv()

    quad = quad_all[...]
    near = choose(low_x, mm(mine_quad, quad), mm(mine_quad, quad, NT))
    apart(quad_exchange.wait_recv)
    their_quad = quad_mixer_in[...]
    mixed = merged(sketch, near, their_quad)

    root_all[pl.ds(pl.multiple_of(shot * tall, tall), tall)] = depth_finish(
        root_sum, root_depth, root_depth_sem, root_own
    )
    @apart
    def _():
        for mask in range(1, shots):
            piece_copy(root_all, shot, root_all_sem, mask).start()

    inverse = inverse_factor(mixed)
    sketch = sketches[3]
    carry = mm(choose(low_y, sketch[:, :rank], sketch[:, rank:]), inverse)
    joined = jnp.concatenate(
        [
            choose(low_x, mine_quad, their_quad),
            choose(low_x, their_quad, mine_quad),
        ],
        axis=1,
    )
    mine_root = mm(carry, joined)
    root_mixer[...] = mine_root
    root_exchange = copy(root_mixer, root_mixer_in, exchange_sem + 1, (flip(4), depth))
    apart(root_exchange.start)

    @apart
    def _():
        for mask in range(1, shots):
            piece_copy(root_all, shot, root_all_sem, mask).wait_recv()

    root = root_all[...]
    near = choose(low_y, mm(mine_root, root), mm(mine_root, root, NT))
    apart(root_exchange.wait_recv)
    their_root = root_mixer_in[...]
    inverse = inverse_factor(merged(sketch, near, their_root))
    mine_root = mm(inverse, mine_root)
    their_root = mm(inverse, their_root)
    mixer = jnp.concatenate(
        [
            choose(low_y, mine_root, their_root),
            choose(low_y, their_root, mine_root),
        ],
        axis=1,
    )

    share_sem = take(2 * shots)
    parts = split(mixer)

    def share_copy(mask, i):
        at = pl.ds(shot * per + 2 * i, 2)
        return copy(gathered.at[at], gathered.at[at], share_sem + 2 * mask + i, (flip(mask), depth))

    def forward_copy(mask, i):
        at = pl.ds(flip(mask) * per + 2 * i, 2)
        return copy(gathered.at[at], gathered.at[at], share_sem + 2 * (mask + 1) + i, (flip(1), depth))

    for i in range(per // 2):
        out = mm3(parts, split(jnp.concatenate([whole[2 * i], whole[2 * i + 1]], axis=1)))
        for w in range(2):
            gathered[shot * per + 2 * i + w] = out[:, w * cells : (w + 1) * cells]

        @apart
        def _():
            for mask in (6, 2, 4, 1):
                share_copy(mask, i).start()

    own = choose(low_x, mine_root[:, : 2 * rank], mine_root[:, 2 * rank :])
    other = choose(low_x, mine_root[:, 2 * rank :], mine_root[:, : 2 * rank])
    near = mm(own, gram)
    near += choose(low_x, mm(other, quad, NT), mm(other, quad))
    far = choose(low_y, mm(their_root, root, NT), mm(their_root, root))
    near += choose(low_x, far[:, : 2 * rank], far[:, 2 * rank :])
    cores[...] = choose(core, near[:, :rank], near[:, rank:]) * (1.0 / math.sqrt(rank))

    def out_copy(row):
        return pltpu.make_async_copy(gathered.at[row], basis.at[:, row], local_sems.at[row])

    def put(mask, i):
        for w in range(2):
            out_copy(flip(mask) * per + 2 * i + w).start()

    @apart
    def _():
        for i in range(per // 2):
            put(0, i)
        for i in range(per // 2):
            for mask in (2, 4, 6):
                share_copy(mask, i).wait_recv()
                forward_copy(mask, i).start()
                put(mask, i)
        for i in range(per // 2):
            for mask in (1, 3, 5, 7):
                share_copy(mask, i).wait_recv()
                put(mask, i)

    @pl.when(depth < depths - 1)
    def _():
        for c in halo_copies(0):
            c.wait_send()

    @pl.when(depth > 0)
    def _():
        for c in halo_copies(1):
            c.wait_send()

    for i in range(shots):
        pair_copy(i).wait_send()
    for mask in range(2, shots):
        spread_copy(flip(mask), mask).wait_send()
    for source, into, sem in (
        (first_sum, first_in, first_sem),
        (quad_sum, quad_depth, quad_depth_sem),
        (root_sum, root_depth, root_depth_sem),
    ):
        for j in range(1, depths):
            other = lax.rem(depth + j, depths)
            copy(source, into.at[depth], sem + j, (shot, other)).wait_send()
    first_pair.wait_send()
    for mask in range(1, shots):
        scatter(quad_part, quad_in, quad_sem, mask).wait_send()
        scatter(root_part, root_in, root_sem, mask).wait_send()
        piece_copy(root_all, shot, root_all_sem, mask).wait_send()
    for mask in range(1, 4):
        piece_copy(quad_all, quad_at, quad_all_sem, mask).wait_send()
    quad_exchange.wait_send()
    root_exchange.wait_send()
    for i in range(per // 2):
        for mask in (1, 2, 4, 6):
            share_copy(mask, i).wait_send()
        for mask in (2, 4, 6):
            forward_copy(mask, i).wait_send()
    for row in range(rows):
        out_copy(row).wait()
    assert used[0] <= SEMS


SEMS = 112


def plane_body(probes, courant, sketches):
    depths = lax.axis_size("depth")
    shots = lax.axis_size("shot")
    local = probes[0]
    rank, rows, cells = local.shape
    per = rows // shots
    tall = rank // 2
    f32 = jnp.float32
    vmem = pl.BlockSpec(memory_space=pltpu.VMEM)
    dma = pltpu.SemaphoreType.DMA

    def scratch(*shape):
        return pltpu.VMEM(shape, f32)

    basis, cores = pl.pallas_call(
        functools.partial(plane_kernel, depths),
        out_shape=(
            jax.ShapeDtypeStruct((rank, rows, cells), f32),
            jax.ShapeDtypeStruct((rank, rank), f32),
        ),
        in_specs=[pl.BlockSpec(memory_space=pl.ANY)] * 3,
        out_specs=(pl.BlockSpec(memory_space=pl.ANY), vmem),
        scratch_shapes=[
            pltpu.VMEM((rank, rows, cells), jnp.bfloat16),
            scratch(rows, cells),
            scratch(shots, rank, 2 * rank),
            scratch(rank * rows, cells),
            pltpu.VMEM((2, STEPS, rank, cells), jnp.bfloat16),
            pltpu.VMEM((2, STEPS, rank, cells), jnp.bfloat16),
            scratch(rows + 2 * STEPS, cells),
            scratch(rows + 2 * STEPS, rank, cells),
            scratch(rows + 2 * STEPS, rank, cells),
            scratch(rows, 2 * rank, cells),
            scratch(per, shots * rank, cells),
            scratch(rank, 2 * rank),
            scratch(depths, rank, 2 * rank),
            scratch(2 * rank, 2 * rank),
            scratch(shots, tall, 2 * rank),
            scratch(shots, tall, 2 * rank),
            scratch(tall, 2 * rank),
            scratch(depths, tall, 2 * rank),
            scratch(2 * rank, 2 * rank),
            scratch(shots, tall, 4 * rank),
            scratch(shots, tall, 4 * rank),
            scratch(tall, 4 * rank),
            scratch(depths, tall, 4 * rank),
            scratch(4 * rank, 4 * rank),
            scratch(rank, 2 * rank),
            scratch(rank, 2 * rank),
            scratch(rank, 4 * rank),
            scratch(rank, 4 * rank),
            scratch(rows, rank, cells),
            dma((SEMS,)),
            dma((SEMS,)),
            dma((rows + 3,)),
        ],
        compiler_params=pltpu.CompilerParams(
            collective_id=0, has_side_effects=True, vmem_limit_bytes=56 * 2**20
        ),
    )(local, courant, jnp.transpose(sketches, (0, 2, 1)))
    return (basis, cores[None])


def solution(mesh):
    placed = (P("shot", None, "depth", None), P("depth", None), P())
    plane = mesh.shape["shot"] == 8
    return jax.shard_map(
        plane_body if plane else body,
        mesh=mesh,
        in_specs=placed,
        out_specs=(P(None, "depth", None), P("shot", None, None)),
        check_vma=False,
    )
```

```python
import functools
import math

import jax
import jax.numpy as jnp
from jax import lax
from jax.experimental import pallas as pl
from jax.experimental.pallas import tpu as pltpu
from jax.sharding import PartitionSpec as P

STEPS = 4
MESH = pl.DeviceIdType.MESH
HI = lax.Precision.HIGHEST
NN = (((1,), (0,)), ((), ()))
NT = (((1,), (1,)), ((), ()))
TN = (((0,), (0,)), ((), ()))
PIECES = 2
WIDTH = 8


def mm(a, b, dims=NN):
    return lax.dot_general(a, b, dims, precision=HI, preferred_element_type=jnp.float32)


def split(x):
    top = x.astype(jnp.bfloat16)
    return top, (x - top.astype(jnp.float32)).astype(jnp.bfloat16)


def mm3(a, b, dims=NN):
    def part(p, q):
        return lax.dot_general(p, q, dims, preferred_element_type=jnp.float32)

    return part(a[0], b[0]) + (part(a[0], b[1]) + part(a[1], b[0]))


def wide(ref, h, d, picked=slice(None)):
    return jnp.concatenate([ref[h, d + i, picked] for i in range(WIDTH)], axis=1)


def inverse_factor(gram):
    n = gram.shape[0]
    rows = lax.broadcasted_iota(jnp.int32, (n, 1), 0)
    eye = (
        lax.broadcasted_iota(jnp.int32, (n, n), 0) == lax.broadcasted_iota(jnp.int32, (n, n), 1)
    ).astype(jnp.float32)
    a = jnp.concatenate([gram, eye], axis=1)
    blocks = [a[8 * b : 8 * b + 8] for b in range(n // 8)]
    inner = lax.broadcasted_iota(jnp.int32, (8, 2 * n), 0)
    for head in range(n // 8):
        columns = {
            b: [
                jnp.broadcast_to(blocks[b][:, 8 * head + j : 8 * head + j + 1], (8, 2 * n))
                for j in range(8)
            ]
            for b in range(head, n // 8)
        }
        for k in range(0, 8, 2):
            if 8 * head + k == n - 2:
                break
            top = columns[head]
            p, q, s = top[k][k : k + 1], top[k][k + 1 : k + 2], top[k + 1][k + 1 : k + 2]
            scale = 1.0 / (p * s - q * q)
            p, q, s = p * scale, q * scale, s * scale

            def solved(x):
                first, second = x[k : k + 1], x[k + 1 : k + 2]
                return s * first - q * second, p * second - q * first

            pivots = {j: solved(top[j]) for j in range(k + 2, 8)}
            row0, row1 = solved(blocks[head])
            for b in range(head if k < 6 else head + 1, n // 8):
                col0, col1 = columns[b][k], columns[b][k + 1]
                if b == head:
                    below = inner > k + 1
                    col0, col1 = jnp.where(below, col0, 0.0), jnp.where(below, col1, 0.0)
                for j, (one, two) in pivots.items():
                    columns[b][j] = columns[b][j] - (col0 * one + col1 * two)
                blocks[b] = blocks[b] - (col0 * row0 + col1 * row1)
    a = jnp.concatenate(blocks, axis=0)
    before = jnp.concatenate([a[n - 1 :], a[: n - 1]], axis=0)
    even = lax.rem(rows, 2) == 0
    own = jnp.sum(a[:, :n] * eye, axis=1, keepdims=True)
    shifted = jnp.concatenate([eye[n - 1 :], eye[: n - 1]], axis=0)
    side = jnp.sum(a[:, :n] * shifted, axis=1, keepdims=True)
    above = jnp.sum(before[:, :n] * shifted, axis=1, keepdims=True)
    ratio = jnp.where(even, 0.0, side / jnp.where(even, 1.0, above))
    value = own - ratio * side
    return (a[:, n:] - ratio * before[:, n:]) * (1.0 / jnp.sqrt(value))


def kernel(
    depths,
    levels,
    probes,
    speed,
    sketches,
    basis,
    cores,
    halo,
    wide_speed,
    field_a,
    field_b,
    pairs,
    sums,
    sums_in,
    halo_send,
    halo_recv,
    speed_send,
    speed_recv,
    pair_send,
    pair_recv,
    sum_send,
    sum_recv,
):
    rows, rank, cells = probes.shape
    shot = lax.axis_index("shot")
    depth = lax.axis_index("depth")
    low_end = depth == 0
    high_end = depth == depths - 1

    def bit(h):
        return lax.rem(shot // (2**h), 2)

    def peer(h):
        return shot + 2**h - 2 ** (h + 1) * bit(h)

    barrier = pltpu.get_barrier_semaphore()
    for h in range(levels):
        pl.semaphore_signal(barrier, inc=1, device_id=(peer(h), depth), device_id_type=MESH)
    for j in range(1, depths):
        other = lax.rem(depth + j, depths)
        pl.semaphore_signal(barrier, inc=1, device_id=(shot, other), device_id_type=MESH)
    pl.semaphore_wait(barrier, levels + depths - 1)

    def halo_copies(side):
        to = depth + 1 if side == 0 else depth - 1
        rows_out = pl.ds(rows - STEPS, STEPS) if side == 0 else pl.ds(0, STEPS)
        first = pltpu.make_async_remote_copy(
            src_ref=probes.at[rows_out],
            dst_ref=halo.at[side],
            send_sem=halo_send.at[side],
            recv_sem=halo_recv.at[side],
            device_id=(shot, to),
            device_id_type=MESH,
        )
        at = 0 if side == 0 else STEPS + rows
        second = pltpu.make_async_remote_copy(
            src_ref=speed.at[rows_out],
            dst_ref=wide_speed.at[pl.ds(at, STEPS)],
            send_sem=speed_send.at[side],
            recv_sem=speed_recv.at[side],
            device_id=(shot, to),
            device_id_type=MESH,
        )
        return first, second

    @pl.when(depth < depths - 1)
    def _():
        for c in halo_copies(0):
            c.start()

    @pl.when(depth > 0)
    def _():
        for c in halo_copies(1):
            c.start()

    @pl.loop(0, rows, unroll=4)
    def _(d):
        field_a[STEPS + d] = probes[d].astype(jnp.float32)

    wide_speed[STEPS : STEPS + rows] = speed[...]

    @pl.when(depth > 0)
    def _():
        for c in halo_copies(0):
            c.wait_recv()
        field_a[0:STEPS] = halo[0].astype(jnp.float32)

    @pl.when(depth == 0)
    def _():
        field_a[0:STEPS] = jnp.zeros((STEPS, rank, cells), jnp.float32)
        wide_speed[0:STEPS] = jnp.zeros((STEPS, cells), jnp.float32)

    @pl.when(depth < depths - 1)
    def _():
        for c in halo_copies(1):
            c.wait_recv()
        field_a[STEPS + rows : 2 * STEPS + rows] = halo[1].astype(jnp.float32)

    @pl.when(depth == depths - 1)
    def _():
        field_a[STEPS + rows : 2 * STEPS + rows] = jnp.zeros((STEPS, rank, cells), jnp.float32)
        wide_speed[STEPS + rows : 2 * STEPS + rows] = jnp.zeros((STEPS, cells), jnp.float32)

    lane = lax.broadcasted_iota(jnp.int32, (rank, cells), 1)
    not_first = lane > 0
    not_last = lane < cells - 1
    me = bit(0)
    mine = pl.ds(pl.multiple_of(me * rank, rank), rank)

    def update(d, source, older):
        u = source[d]
        left = jnp.where(not_first, pltpu.roll(u, 1, 1), 0.0)
        right = jnp.where(not_last, pltpu.roll(u, cells - 1, 1), 0.0)
        laplace = source[d + 1] + source[d - 1] + right + left - 4.0 * u
        return 2.0 * u - older + wide_speed[pl.ds(d, 1)] * laplace

    for step in range(STEPS):
        source, target = (field_a, field_b) if step % 2 == 0 else (field_b, field_a)
        last = step == STEPS - 1

        @pl.loop(step + 1, 2 * STEPS + rows - step - 1, unroll=2)
        def _(d):
            older = source[d] if step == 0 else target[d]
            new = update(d, source, older)
            if last:
                pairs[0, d - STEPS, mine] = new
            else:
                target[d] = new

    def pair_copy(h):
        own = pl.ds(pl.multiple_of(bit(h) * rank, rank), rank)
        return [
            pltpu.make_async_remote_copy(
                src_ref=pairs.at[h, :, own],
                dst_ref=pairs.at[h, :, own],
                send_sem=pair_send.at[h, 0, 0],
                recv_sem=pair_recv.at[h, 0, 0],
                device_id=(peer(h), depth),
                device_id_type=MESH,
            )
        ]

    for c in pair_copy(0):
        c.start()
    for c in pair_copy(0):
        c.wait()

    def gram_body(d, total):
        x = split(wide(pairs, 0, d * WIDTH))
        return total + mm3(x, x, NT)

    zero = jnp.zeros((2 * rank, 2 * rank), jnp.float32)
    gram = lax.fori_loop(0, rows // WIDTH, gram_body, zero)

    def sum_copy(h, j):
        other = lax.rem(depth + j, depths)
        size = 2 * rank if h == 0 else rank
        return pltpu.make_async_remote_copy(
            src_ref=sums.at[h, pl.ds(0, size)],
            dst_ref=sums_in.at[h, depth, pl.ds(0, size)],
            send_sem=sum_send.at[h, j],
            recv_sem=sum_recv.at[h, j],
            device_id=(shot, other),
            device_id_type=MESH,
        )

    def depth_sum(h, value):
        size = value.shape[0]
        sums[h, 0:size] = value
        for j in range(1, depths):
            sum_copy(h, j).start()
        for j in range(1, depths):
            sum_copy(h, j).wait()
        total = None
        for j in range(depths):
            part = jnp.where(depth == j, value, sums_in[h, j, 0:size])
            total = part if total is None else total + part
        return total

    for h in range(levels):
        sums_in[h, depth] = jnp.zeros((2 * rank, 2 * rank), jnp.float32)
    gram = depth_sum(0, gram)

    low = inverse_factor(gram[:rank, :rank])
    high = inverse_factor(gram[rank:, rank:])
    sketch = sketches[shot // 2 * 2]
    mixer = jnp.concatenate(
        [mm(sketch[:rank], low, TN), mm(sketch[rank:], high, TN)], axis=1
    )
    carried = mm(mixer, gram)
    inverse = inverse_factor(mm(carried, mixer, NT))
    mixer = mm(inverse, mixer)
    carried = mm(inverse, carried)
    projected = jnp.where(me == 0, carried[:, :rank], carried[:, rank:])

    for h in range(1, levels):
        own_bit = bit(h)
        own = pl.ds(pl.multiple_of(own_bit * rank, rank), rank)

        parts = split(mixer)
        part_rows = rows // 2**h
        per = part_rows // PIECES
        got = pl.ds(pl.multiple_of((1 - own_bit) * rank, rank), rank)

        def part_at(mask, i):
            part = 0
            for b in range(h):
                part += 2**b * (1 - bit(b) if mask >> b & 1 else bit(b))
            return pl.ds(part * part_rows + i * per, per)

        def part_copy(mask, i):
            low = mask & -mask
            at = part_at(mask - low, i)
            lanes = got if mask else own
            return pltpu.make_async_remote_copy(
                src_ref=pairs.at[h, at, lanes],
                dst_ref=pairs.at[h, at, lanes],
                send_sem=pair_send.at[h, mask, i],
                recv_sem=pair_recv.at[h, mask, i],
                device_id=(peer(low.bit_length() - 1 if mask else h), depth),
                device_id_type=MESH,
            )

        chunks = rows // WIDTH
        ahead = max(1, part_rows // WIDTH)
        first = part_at(0, 0).start // WIDTH
        for t in range(chunks):
            at = lax.rem(first + t, chunks) * WIDTH
            out = mm3(parts, split(wide(pairs, h - 1, at)))
            for w in range(WIDTH):
                pairs[h, at + w, own] = out[:, w * cells : (w + 1) * cells]
            if per == WIDTH and t < PIECES:
                part_copy(0, t).start()
            elif per != WIDTH and t == ahead - 1:
                for i in range(PIECES):
                    part_copy(0, i).start()
        masks = sorted(range(2**h), key=lambda m: (m.bit_count(), -m))
        for mask in masks:
            low = mask & -mask if mask else 2**h
            for i in range(PIECES):
                part_copy(mask, i).wait_recv()
                for b in reversed(range(low.bit_length() - 1)):
                    part_copy(mask + 2**b, i).start()
        for mask in masks:
            for i in range(PIECES):
                part_copy(mask, i).wait_send()

        def cross_body(d, total):
            y = split(wide(pairs, h, d * WIDTH))
            r = split(wide(pairs, 0, d * WIDTH, mine))
            right = [jnp.concatenate([p[rank:], q], axis=0) for p, q in zip(y, r)]
            return total + mm3(y, right, NT)

        cross = lax.fori_loop(0, rows // WIDTH, cross_body, zero)
        value = jnp.concatenate(
            [
                cross[:rank, :rank],
                jnp.where(own_bit == 0, cross[rank:, rank:], cross[:rank, rank:]),
            ],
            axis=1,
        )
        value = depth_sum(h, value)
        stride = 2**h
        sketch = sketches[shot // (2 * stride) * (2 * stride) + stride - 1]
        top, bottom = sketch[:rank], sketch[rank:]
        across = value[:, :rank]
        mixed = mm(sketch, sketch, TN)
        mixed += mm(top, mm(across, bottom), TN) + mm(bottom, mm(across, top, TN), TN)
        inverse = inverse_factor(mixed)
        mixer = mm(inverse, sketch, NT)
        other = value[:, rank:]
        low_part = jnp.where(own_bit == 0, projected, other)
        high_part = jnp.where(own_bit == 0, other, projected)
        projected = mm(mixer, jnp.concatenate([low_part, high_part], axis=0))

    parts = split(mixer)

    @pl.loop(0, rows // WIDTH)
    def _(i):
        out = mm3(parts, split(wide(pairs, levels - 1, i * WIDTH)))
        for w in range(WIDTH):
            basis[i * WIDTH + w] = out[:, w * cells : (w + 1) * cells]

    cores[...] = projected * (1.0 / math.sqrt(rank))

    @pl.when(depth < depths - 1)
    def _():
        for c in halo_copies(0):
            c.wait_send()

    @pl.when(depth > 0)
    def _():
        for c in halo_copies(1):
            c.wait_send()


def body(probes, courant, sketches):
    depths = lax.axis_size("depth")
    levels = lax.axis_size("shot").bit_length() - 1
    local = jnp.transpose(probes[0], (1, 0, 2))
    rows, rank, cells = local.shape
    f32 = jnp.float32
    vmem = pl.BlockSpec(memory_space=pltpu.VMEM)
    dma = pltpu.SemaphoreType.DMA
    basis, cores = pl.pallas_call(
        functools.partial(kernel, depths, levels),
        out_shape=(
            jax.ShapeDtypeStruct((rows, rank, cells), f32),
            jax.ShapeDtypeStruct((rank, rank), f32),
        ),
        in_specs=[vmem] * 3,
        out_specs=(vmem, vmem),
        scratch_shapes=[
            pltpu.VMEM((2, STEPS, rank, cells), jnp.bfloat16),
            pltpu.VMEM((rows + 2 * STEPS, cells), f32),
            pltpu.VMEM((rows + 2 * STEPS, rank, cells), f32),
            pltpu.VMEM((rows + 2 * STEPS, rank, cells), f32),
            pltpu.VMEM((levels, rows, 2 * rank, cells), f32),
            pltpu.VMEM((levels, 2 * rank, 2 * rank), f32),
            pltpu.VMEM((levels, depths, 2 * rank, 2 * rank), f32),
            dma((2,)),
            dma((2,)),
            dma((2,)),
            dma((2,)),
            dma((levels, 2 ** (levels - 1), PIECES)),
            dma((levels, 2 ** (levels - 1), PIECES)),
            dma((levels, depths)),
            dma((levels, depths)),
        ],
        compiler_params=pltpu.CompilerParams(
            collective_id=0, has_side_effects=True, vmem_limit_bytes=56 * 2**20
        ),
    )(local, courant, sketches)
    return (jnp.transpose(basis, (1, 0, 2)), cores[None])


def choose(bit_value, low, high):
    return jnp.where(bit_value == 0, low, high)


def merged(sketch, near, theirs):
    half = mm(
        jnp.concatenate([0.5 * sketch, near], axis=1),
        jnp.concatenate([sketch, theirs], axis=1),
        NT,
    )
    return half + jnp.transpose(half)


def plane_kernel(
    depths,
    probes_in,
    speed_in,
    sketches_in,
    basis,
    cores,
    probes,
    speed,
    sketches,
    flat,
    edges,
    halo,
    wide_speed,
    field_a,
    field_b,
    pair,
    whole,
    first_sum,
    first_in,
    gram_all,
    quad_part,
    quad_in,
    quad_sum,
    quad_depth,
    quad_all,
    root_part,
    root_in,
    root_sum,
    root_depth,
    root_all,
    quad_mixer,
    quad_mixer_in,
    root_mixer,
    root_mixer_in,
    gathered,
    send_sems,
    recv_sems,
    local_sems,
):
    rank, rows, cells = probes.shape
    shots = 8
    per = rows // shots
    part = 2 * rank // 4
    shot = lax.axis_index("shot")
    depth = lax.axis_index("depth")

    def bit(h, of=shot):
        return lax.rem(of // (2**h), 2)

    def flip(mask, of=shot):
        value = 0
        for h in range(3):
            value += 2**h * (1 - bit(h, of) if mask >> h & 1 else bit(h, of))
        return value

    core, low_x, low_y = bit(0), bit(1), bit(2)

    barrier = pltpu.get_barrier_semaphore()
    for mask in range(1, shots):
        pl.semaphore_signal(barrier, inc=1, device_id=(flip(mask), depth), device_id_type=MESH)
    for j in range(1, depths):
        other = lax.rem(depth + j, depths)
        pl.semaphore_signal(barrier, inc=1, device_id=(shot, other), device_id_type=MESH)

    loads = [
        pltpu.make_async_copy(probes_in, probes, local_sems.at[rows]),
        pltpu.make_async_copy(speed_in, speed, local_sems.at[rows + 1]),
        pltpu.make_async_copy(sketches_in, sketches, local_sems.at[rows + 2]),
    ]
    for c in loads:
        c.start()
    loads[0].wait()

    @pl.loop(0, rank, unroll=4)
    def _(i):
        at = pl.ds(pl.multiple_of(i * rows, rows), rows)
        flat[at] = probes[i].astype(jnp.float32)

    @pl.loop(0, rows, unroll=4)
    def _(d):
        field_a[STEPS + d] = flat[pl.ds(d, rank, stride=rows)]

    for d in range(STEPS):
        edges[0, d] = field_a[rows + d].astype(jnp.bfloat16)
        edges[1, d] = field_a[STEPS + d].astype(jnp.bfloat16)
    loads[1].wait()
    wide_speed[STEPS : STEPS + rows] = speed[...]

    @pl.loop(0, 1 + shot // shots)
    def _(_):
        pl.semaphore_wait(barrier, shots - 1 + depths - 1)

    used = [0]

    def apart(work):
        @pl.loop(0, 1 + shot // shots)
        def _(_):
            work()

    def take(count):
        used[0] += count
        return used[0] - count

    def copy(src, dst, sem, to):
        return pltpu.make_async_remote_copy(
            src_ref=src,
            dst_ref=dst,
            send_sem=send_sems.at[sem],
            recv_sem=recv_sems.at[sem],
            device_id=to,
            device_id_type=MESH,
        )

    halo_sem, speed_sem = take(2), take(2)

    def halo_copies(side):
        to = depth + 1 if side == 0 else depth - 1
        rows_out = pl.ds(rows - STEPS, STEPS) if side == 0 else pl.ds(0, STEPS)
        at = 0 if side == 0 else STEPS + rows
        return (
            copy(edges.at[side], halo.at[side], halo_sem + side, (shot, to)),
            copy(
                speed.at[rows_out],
                wide_speed.at[pl.ds(at, STEPS)],
                speed_sem + side,
                (shot, to),
            ),
        )

    @pl.when(depth < depths - 1)
    def _():
        for c in halo_copies(0):
            c.start()

    @pl.when(depth > 0)
    def _():
        for c in halo_copies(1):
            c.start()

    @pl.when(depth > 0)
    def _():
        for c in halo_copies(0):
            c.wait_recv()
        field_a[0:STEPS] = halo[0].astype(jnp.float32)

    @pl.when(depth == 0)
    def _():
        field_a[0:STEPS] = jnp.zeros((STEPS, rank, cells), jnp.float32)
        wide_speed[0:STEPS] = jnp.zeros((STEPS, cells), jnp.float32)

    @pl.when(depth < depths - 1)
    def _():
        for c in halo_copies(1):
            c.wait_recv()
        field_a[STEPS + rows : 2 * STEPS + rows] = halo[1].astype(jnp.float32)

    @pl.when(depth == depths - 1)
    def _():
        field_a[STEPS + rows : 2 * STEPS + rows] = jnp.zeros((STEPS, rank, cells), jnp.float32)
        wide_speed[STEPS + rows : 2 * STEPS + rows] = jnp.zeros((STEPS, cells), jnp.float32)

    lane = lax.broadcasted_iota(jnp.int32, (rank, cells), 1)
    not_first = lane > 0
    not_last = lane < cells - 1
    mine = pl.ds(pl.multiple_of(core * rank, rank), rank)

    def update(d, source, older):
        u = source[d]
        left = jnp.where(not_first, pltpu.roll(u, 1, 1), 0.0)
        right = jnp.where(not_last, pltpu.roll(u, cells - 1, 1), 0.0)
        laplace = source[d + 1] + source[d - 1] + right + left - 4.0 * u
        return 2.0 * u - older + wide_speed[pl.ds(d, 1)] * laplace

    for step in range(STEPS - 1):
        source, target = (field_a, field_b) if step % 2 == 0 else (field_b, field_a)

        @pl.loop(step + 1, 2 * STEPS + rows - step - 1, unroll=2)
        def _(d):
            older = source[d] if step == 0 else target[d]
            target[d] = update(d, source, older)

    pair_sem, spread_sem = take(shots), take(shots)

    def pair_copy(i):
        at = pl.ds(i * per, per)
        return copy(pair.at[at, mine], pair.at[at, mine], pair_sem + i, (flip(1), depth))

    def spread_copy(to, mask):
        at = pl.ds(to * per, per)
        into = pl.ds(pl.multiple_of(shot * rank, rank), rank)
        return copy(pair.at[at, mine], whole.at[:, into], spread_sem + mask, (to, depth))

    source, target = (field_a, field_b) if (STEPS - 1) % 2 == 0 else (field_b, field_a)

    @pl.loop(0, shots)
    def _(i):
        for w in range(per):
            d = STEPS + i * per + w
            pair[i * per + w, mine] = update(d, source, target[d])
        pair_copy(i).start()

        @pl.when(i // 2 != shot // 2)
        def _():
            mask = 0
            for h in range(3):
                mask += 2**h * lax.rem(bit(h, i) + bit(h), 2)
            spread_copy(i, mask).start()

    group = WIDTH // per

    def gram_body(t, total):
        for i in range(group):
            pair_copy(t * group + i).wait_recv()
        at = t * WIDTH
        x = split(jnp.concatenate([pair[at + i] for i in range(WIDTH)], axis=1))
        return total + mm3(x, x, NT)

    zero = jnp.zeros((2 * rank, 2 * rank), jnp.float32)
    gram = lax.fori_loop(0, rows // WIDTH, gram_body, zero)

    def depth_start(source, into, sem):
        @apart
        def _():
            for j in range(1, depths):
                other = lax.rem(depth + j, depths)
                copy(source, into.at[depth], sem + j, (shot, other)).start()

    def depth_finish(source, into, sem, value):
        @apart
        def _():
            for j in range(1, depths):
                other = lax.rem(depth + j, depths)
                copy(source, into.at[depth], sem + j, (shot, other)).wait_recv()

        total = None
        for j in range(depths):
            one = jnp.where(depth == j, value, into[j])
            total = one if total is None else total + one
        return total

    for into in (first_in, quad_depth, root_depth):
        into[depth] = jnp.zeros(into.shape[1:], jnp.float32)

    first_sem, first_pair_sem = take(depths), take(1)
    half = choose(core, gram[:rank], gram[rank:])
    first_sum[...] = half
    depth_start(first_sum, first_in, first_sem)
    own_rows = pl.ds(pl.multiple_of(shot // 2 * 2 * rank, 2 * rank), 2 * rank)
    for w in range(per):
        whole[w, own_rows] = pair[shot * per + w]
    gram_all[mine] = depth_finish(first_sum, first_in, first_sem, half)
    first_pair = copy(gram_all.at[mine], gram_all.at[mine], first_pair_sem, (flip(1), depth))
    apart(first_pair.start)
    apart(first_pair.wait_recv)
    gram = gram_all[...]

    loads[2].wait()
    low = inverse_factor(gram[:rank, :rank])
    high = inverse_factor(gram[rank:, rank:])

    sketch = sketches[shot // 2 * 2]
    left = mm(sketch[:, :rank], low)
    right = mm(sketch[:, rank:], high)
    mixed = merged(sketch, mm(left, gram[:rank, rank:]), right)

    inverse = inverse_factor(mixed)
    sketch = sketches[shot // 4 * 4 + 1]
    carry = mm(choose(low_x, sketch[:, :rank], sketch[:, rank:]), inverse)
    mine_quad = mm(carry, jnp.concatenate([left, right], axis=1))
    quad_mixer[...] = mine_quad
    exchange_sem = take(2)
    quad_exchange = copy(quad_mixer, quad_mixer_in, exchange_sem, (flip(2), depth))
    apart(quad_exchange.start)

    @apart
    def _():
        for mask in range(2, shots):
            spread_copy(flip(mask), mask).wait_recv()

    def cross(first, second, size):
        total = None
        for w in range(0, per, 2):
            x = split(jnp.concatenate([whole[w, first : first + size], whole[w + 1, first : first + size]], axis=1))
            y = split(jnp.concatenate([whole[w, second : second + size], whole[w + 1, second : second + size]], axis=1))
            one = mm3(x, y, NT)
            total = one if total is None else total + one
        return total

    quad_sem, quad_depth_sem, quad_all_sem = take(shots), take(depths), take(4)
    root_sem, root_depth_sem, root_all_sem = take(shots), take(depths), take(shots)
    tall = 2 * rank // 4
    for q in range(2):
        value = cross(4 * rank * q, 4 * rank * q + 2 * rank, 2 * rank)
        for i in range(4):
            quad_part[4 * q + i] = value[i * tall : (i + 1) * tall]

    def scatter(source, into, sem, mask):
        return copy(source.at[flip(mask)], into.at[mask], sem + mask, (flip(mask), depth))

    @apart
    def _():
        for mask in range(1, shots):
            scatter(quad_part, quad_in, quad_sem, mask).start()

    value = cross(0, 4 * rank, 4 * rank)
    for i in range(shots):
        root_part[i] = value[i * tall : (i + 1) * tall]
    @apart
    def _():
        for mask in range(1, shots):
            scatter(root_part, root_in, root_sem, mask).start()

    def scattered(source, into, sem):
        @apart
        def _():
            for mask in range(1, shots):
                scatter(source, into, sem, mask).wait_recv()

        total = source[shot]
        for mask in range(1, shots):
            total = total + into[mask]
        return total

    def piece_copy(ref, at, sem, mask):
        here = pl.ds(pl.multiple_of(at * tall, tall), tall)
        return copy(ref.at[here], ref.at[here], sem + mask, (flip(mask), depth))

    quad_own = scattered(quad_part, quad_in, quad_sem)
    quad_sum[...] = quad_own
    depth_start(quad_sum, quad_depth, quad_depth_sem)

    root_own = scattered(root_part, root_in, root_sem)
    root_sum[...] = root_own
    depth_start(root_sum, root_depth, root_depth_sem)
    quad_at = 2 * low_x + core
    quad_all[pl.ds(pl.multiple_of(quad_at * tall, tall), tall)] = depth_finish(
        quad_sum, quad_depth, quad_depth_sem, quad_own
    )
    @apart
    def _():
        for mask in range(1, 4):
            piece_copy(quad_all, quad_at, quad_all_sem, mask).start()

    @apart
    def _():
        for mask in range(1, 4):
            piece_copy(quad_all, quad_at, quad_all_sem, mask).wait_recv()

    quad = quad_all[...]
    near = choose(low_x, mm(mine_quad, quad), mm(mine_quad, quad, NT))
    apart(quad_exchange.wait_recv)
    their_quad = quad_mixer_in[...]
    mixed = merged(sketch, near, their_quad)

    root_all[pl.ds(pl.multiple_of(shot * tall, tall), tall)] = depth_finish(
        root_sum, root_depth, root_depth_sem, root_own
    )
    @apart
    def _():
        for mask in range(1, shots):
            piece_copy(root_all, shot, root_all_sem, mask).start()

    inverse = inverse_factor(mixed)
    sketch = sketches[3]
    carry = mm(choose(low_y, sketch[:, :rank], sketch[:, rank:]), inverse)
    joined = jnp.concatenate(
        [
            choose(low_x, mine_quad, their_quad),
            choose(low_x, their_quad, mine_quad),
        ],
        axis=1,
    )
    mine_root = mm(carry, joined)
    root_mixer[...] = mine_root
    root_exchange = copy(root_mixer, root_mixer_in, exchange_sem + 1, (flip(4), depth))
    apart(root_exchange.start)

    @apart
    def _():
        for mask in range(1, shots):
            piece_copy(root_all, shot, root_all_sem, mask).wait_recv()

    root = root_all[...]
    near = choose(low_y, mm(mine_root, root), mm(mine_root, root, NT))
    apart(root_exchange.wait_recv)
    their_root = root_mixer_in[...]
    inverse = inverse_factor(merged(sketch, near, their_root))
    mine_root = mm(inverse, mine_root)
    their_root = mm(inverse, their_root)
    mixer = jnp.concatenate(
        [
            choose(low_y, mine_root, their_root),
            choose(low_y, their_root, mine_root),
        ],
        axis=1,
    )

    share_sem = take(2 * shots)
    parts = split(mixer)

    def share_copy(mask, i):
        at = pl.ds(shot * per + 2 * i, 2)
        return copy(gathered.at[at], gathered.at[at], share_sem + 2 * mask + i, (flip(mask), depth))

    def forward_copy(mask, i):
        at = pl.ds(flip(mask) * per + 2 * i, 2)
        return copy(gathered.at[at], gathered.at[at], share_sem + 2 * (mask + 1) + i, (flip(1), depth))

    for i in range(per // 2):
        out = mm3(parts, split(jnp.concatenate([whole[2 * i], whole[2 * i + 1]], axis=1)))
        for w in range(2):
            gathered[shot * per + 2 * i + w] = out[:, w * cells : (w + 1) * cells]

        @apart
        def _():
            for mask in (6, 2, 4, 1):
                share_copy(mask, i).start()

    own = choose(low_x, mine_root[:, : 2 * rank], mine_root[:, 2 * rank :])
    other = choose(low_x, mine_root[:, 2 * rank :], mine_root[:, : 2 * rank])
    near = mm(own, gram)
    near += choose(low_x, mm(other, quad, NT), mm(other, quad))
    far = choose(low_y, mm(their_root, root, NT), mm(their_root, root))
    near += choose(low_x, far[:, : 2 * rank], far[:, 2 * rank :])
    cores[...] = choose(core, near[:, :rank], near[:, rank:]) * (1.0 / math.sqrt(rank))

    def out_copy(row):
        return pltpu.make_async_copy(gathered.at[row], basis.at[:, row], local_sems.at[row])

    def put(mask, i):
        for w in range(2):
            out_copy(flip(mask) * per + 2 * i + w).start()

    @apart
    def _():
        for i in range(per // 2):
            put(0, i)
        for i in range(per // 2):
            for mask in (2, 4, 6):
                share_copy(mask, i).wait_recv()
                forward_copy(mask, i).start()
                put(mask, i)
        for i in range(per // 2):
            for mask in (1, 3, 5, 7):
                share_copy(mask, i).wait_recv()
                put(mask, i)

    @pl.when(depth < depths - 1)
    def _():
        for c in halo_copies(0):
            c.wait_send()

    @pl.when(depth > 0)
    def _():
        for c in halo_copies(1):
            c.wait_send()

    for i in range(shots):
        pair_copy(i).wait_send()
    for mask in range(2, shots):
        spread_copy(flip(mask), mask).wait_send()
    for source, into, sem in (
        (first_sum, first_in, first_sem),
        (quad_sum, quad_depth, quad_depth_sem),
        (root_sum, root_depth, root_depth_sem),
    ):
        for j in range(1, depths):
            other = lax.rem(depth + j, depths)
            copy(source, into.at[depth], sem + j, (shot, other)).wait_send()
    first_pair.wait_send()
    for mask in range(1, shots):
        scatter(quad_part, quad_in, quad_sem, mask).wait_send()
        scatter(root_part, root_in, root_sem, mask).wait_send()
        piece_copy(root_all, shot, root_all_sem, mask).wait_send()
    for mask in range(1, 4):
        piece_copy(quad_all, quad_at, quad_all_sem, mask).wait_send()
    quad_exchange.wait_send()
    root_exchange.wait_send()
    for i in range(per // 2):
        for mask in (1, 2, 4, 6):
            share_copy(mask, i).wait_send()
        for mask in (2, 4, 6):
            forward_copy(mask, i).wait_send()
    for row in range(rows):
        out_copy(row).wait()
    assert used[0] <= SEMS


SEMS = 112


def plane_body(probes, courant, sketches):
    depths = lax.axis_size("depth")
    shots = lax.axis_size("shot")
    local = probes[0]
    rank, rows, cells = local.shape
    per = rows // shots
    tall = rank // 2
    f32 = jnp.float32
    vmem = pl.BlockSpec(memory_space=pltpu.VMEM)
    dma = pltpu.SemaphoreType.DMA

    def scratch(*shape):
        return pltpu.VMEM(shape, f32)

    basis, cores = pl.pallas_call(
        functools.partial(plane_kernel, depths),
        out_shape=(
            jax.ShapeDtypeStruct((rank, rows, cells), f32),
            jax.ShapeDtypeStruct((rank, rank), f32),
        ),
        in_specs=[pl.BlockSpec(memory_space=pl.ANY)] * 3,
        out_specs=(pl.BlockSpec(memory_space=pl.ANY), vmem),
        scratch_shapes=[
            pltpu.VMEM((rank, rows, cells), jnp.bfloat16),
            scratch(rows, cells),
            scratch(shots, rank, 2 * rank),
            scratch(rank * rows, cells),
            pltpu.VMEM((2, STEPS, rank, cells), jnp.bfloat16),
            pltpu.VMEM((2, STEPS, rank, cells), jnp.bfloat16),
            scratch(rows + 2 * STEPS, cells),
            scratch(rows + 2 * STEPS, rank, cells),
            scratch(rows + 2 * STEPS, rank, cells),
            scratch(rows, 2 * rank, cells),
            scratch(per, shots * rank, cells),
            scratch(rank, 2 * rank),
            scratch(depths, rank, 2 * rank),
            scratch(2 * rank, 2 * rank),
            scratch(shots, tall, 2 * rank),
            scratch(shots, tall, 2 * rank),
            scratch(tall, 2 * rank),
            scratch(depths, tall, 2 * rank),
            scratch(2 * rank, 2 * rank),
            scratch(shots, tall, 4 * rank),
            scratch(shots, tall, 4 * rank),
            scratch(tall, 4 * rank),
            scratch(depths, tall, 4 * rank),
            scratch(4 * rank, 4 * rank),
            scratch(rank, 2 * rank),
            scratch(rank, 2 * rank),
            scratch(rank, 4 * rank),
            scratch(rank, 4 * rank),
            scratch(rows, rank, cells),
            dma((SEMS,)),
            dma((SEMS,)),
            dma((rows + 3,)),
        ],
        compiler_params=pltpu.CompilerParams(
            collective_id=0, has_side_effects=True, vmem_limit_bytes=56 * 2**20
        ),
    )(local, courant, jnp.transpose(sketches, (0, 2, 1)))
    return (basis, cores[None])


def solution(mesh):
    placed = (P("shot", None, "depth", None), P("depth", None), P())
    plane = mesh.shape["shot"] == 8
    return jax.shard_map(
        plane_body if plane else body,
        mesh=mesh,
        in_specs=placed,
        out_specs=(P(None, "depth", None), P("shot", None, None)),
        check_vma=False,
    )
```
